128 devices in a mesh: inner: 32 (over z_lo, x, y), outer: 4 (over z_hi, core).
Axes of the slice: x: 4, y: 4, z: 4 (z_hi: 2, z_lo: 2; z = z_hi * 2 + z_lo), core: 2. Of those that a mesh axis runs over, the one named last changes fastest.
Arguments:
- hidden: bfloat16 [32768, 1152], P(('inner', 'outer')), may hold values from -6 to 6
- latents_now: float32 [128, 16, 256], P(('inner', 'outer')), may hold values from -6 to 6
- latents_next: float32 [128, 16, 256], P(('inner', 'outer')), may hold values from -6.3 to 6.3
- timestep: int32 [1], replicated, may hold values from 3 to 9
- version_tags: int32 [128], P(('inner', 'outer')), may hold values from 0 to 7
- noise_levels: float32 [8], replicated, may hold values from 0.5 to 1
- time_weight: bfloat16 [256, 6912], replicated, may hold values from -0.375 to 0.375
- spatial_qkv: bfloat16 [1152, 3456], replicated, may hold values from -0.1875 to 0.1875
- spatial_out: bfloat16 [1152, 1152], replicated, may hold values from -0.1875 to 0.1875
- temporal_qkv: bfloat16 [1152, 3456], replicated, may hold values from -0.1875 to 0.1875
- temporal_out: bfloat16 [1152, 1152], replicated, may hold values from -0.1875 to 0.1875
- final_weight: bfloat16 [16, 1152], replicated, may hold values from -0.1875 to 0.1875
Outputs:
- log_prob: float32 [128, 256], P(('inner', 'outer'))
- next_mean: float32 [128, 16, 256], P(('inner', 'outer'))
The draws below stay inside these ranges and needn't reach their ends.
Inputs may be any that keep to these rules, and one draw needn't show every extreme that they name: `timestep`: the index k of the denoising step, whose time is k / 10.
All inputs are finite; a program needn't handle non-finite values.
Results may differ from the reference program's by a relative error of at most 0.004.
Values may be sent and summed in bfloat16 or wider, within the bound.
No kernel may reach another device: no remote copies, remote signals or barrier semaphores. Data moves between devices by JAX's collectives and lax.ppermute only.
A program may use at most 128 MiB of HBM per device.

```python
import math
import jax
import jax.numpy as jnp
from jax import lax

D = 1152
HEADS = 16
C = 16
FREQ = 256
STEPS = 10
VERSIONS = 8
TPF = 256
FRAMES = 128
TOKENS = 32768


def latent_pair(key):
    first_key = jax.random.fold_in(key, 11)
    second_key = jax.random.fold_in(key, 12)
    shape = (FRAMES, C, TPF)
    current = jnp.clip(jax.random.normal(first_key, shape, jnp.float32), -6.0, 6.0)
    jitter = jnp.clip(jax.random.normal(second_key, shape, jnp.float32), -6.0, 6.0)
    return (current, current + 0.05 * jitter)


def draw_latents_now(key, part):
    return latent_pair(key)[0]


def draw_latents_next(key, part):
    return latent_pair(key)[1]


def place_ends(result, own_key, low, top_value):
    longest = result.shape.index(max(result.shape))
    spots = []
    for shift in (0, 1):
        where = [jax.random.randint(jax.random.fold_in(own_key, axis), (), 0, length) for axis, length in enumerate(result.shape)]
        where[longest] = (where[longest] + shift) % result.shape[longest]
        spots.append(tuple(where))
    return result.at[spots[0]].set(low).at[spots[1]].set(top_value)


def block_levels(rng, dims, shards, smallest, largest):
    loudness = 1.0
    for dim, shards_of in shards:
        draws = jax.random.uniform(jax.random.fold_in(jax.random.fold_in(rng, 6), dim), (shards_of,), jnp.float32, smallest / len(shards), largest / len(shards))
        loudness = loudness * jnp.repeat(jnp.exp(draws), dims[dim] // shards_of).reshape((-1,) + (1,) * (len(dims) - 1 - dim))
    return loudness


def noise(rng, extent, deviation, limit, split=(), kind=jnp.bfloat16):
    array = deviation * jax.random.normal(rng, extent, jnp.float32)
    if split:
        array = array * block_levels(rng, extent, split, -0.22, 0.18)
    return jnp.clip(array, -limit, limit).astype(kind)


def setup_inputs(seed: int = 0) -> dict:
    keys = jax.random.split(jax.random.key(seed), 13)
    hidden = noise(keys[0], (TOKENS, D), 1.0, 6.0, ((0, 128),))
    latents_now = draw_latents_now(jax.random.fold_in(keys[12], 71), 0)
    latents_next = draw_latents_next(jax.random.fold_in(keys[12], 71), 0)
    timestep = jax.random.randint(keys[3], (1,), 3, STEPS).astype(jnp.int32)
    version_tags = place_ends(jax.random.randint(keys[4], (FRAMES,), 0, VERSIONS), jax.random.fold_in(keys[4], 1), 0, VERSIONS - 1).astype(jnp.int32)
    noise_levels = jnp.clip(jnp.exp(jax.random.uniform(keys[5], (VERSIONS,), jnp.float32, math.log(0.5), math.log(1.0))), 0.5, 1.0)
    time_weight = noise(keys[6], (FREQ, 6 * D), FREQ ** -0.5, 0.375)
    spatial_qkv = noise(keys[7], (D, 3 * D), D ** -0.5, 0.1875)
    spatial_out = noise(keys[8], (D, D), D ** -0.5, 0.1875)
    temporal_qkv = noise(keys[9], (D, 3 * D), D ** -0.5, 0.1875)
    temporal_out = noise(keys[10], (D, D), D ** -0.5, 0.1875)
    final_weight = noise(keys[11], (C, D), D ** -0.5, 0.1875)
    return dict(hidden=hidden, latents_now=latents_now, latents_next=latents_next, timestep=timestep, version_tags=version_tags, noise_levels=noise_levels, time_weight=time_weight, spatial_qkv=spatial_qkv, spatial_out=spatial_out, temporal_qkv=temporal_qkv, temporal_out=temporal_out, final_weight=final_weight)


norm_eps = 1e-06

def layer_norm(values):
    average = lax.optimization_barrier(jnp.mean(values, -1, keepdims=True))
    centred = values - average
    variance = lax.optimization_barrier(jnp.mean(centred * centred, -1, keepdims=True))
    return centred * lax.rsqrt(variance + norm_eps)

def head_norm(values):
    return values * lax.rsqrt(lax.optimization_barrier(jnp.mean(values * values, -1, keepdims=True)) + norm_eps)

def modulation(timestep, time_weight):
    half_width = FREQ // 2
    time_value = timestep.astype(jnp.float32) / STEPS
    frequencies = jnp.exp(-math.log(10000.0) * jnp.arange(half_width).astype(jnp.float32) / half_width)
    angles = 1000.0 * time_value[:, None] * frequencies[None, :]
    embedded = jnp.concatenate([jnp.cos(angles), jnp.sin(angles)], 1)
    activated = jax.nn.silu(embedded).astype(jnp.bfloat16)
    return jnp.dot(activated, time_weight, preferred_element_type=jnp.float32)[0]

def heads_of(normed, qkv_weight):
    rows = normed.shape[0]
    head_width = D // HEADS
    mixed = jnp.dot(normed, qkv_weight, preferred_element_type=jnp.float32)
    queries = head_norm(mixed[:, :D].reshape(rows, HEADS, head_width)) * head_width ** (-0.5)
    key_rows = head_norm(mixed[:, D:2 * D].reshape(rows, HEADS, head_width))
    value_rows = mixed[:, 2 * D:].reshape(rows, HEADS, head_width)
    return (queries.astype(jnp.bfloat16), key_rows.astype(jnp.bfloat16), value_rows.astype(jnp.bfloat16))

def attend(queries, key_rows, value_rows):
    scores = jnp.einsum('qhe,khe->hqk', queries.astype(jnp.float32), key_rows.astype(jnp.float32))
    weights = jnp.exp(scores)
    weights = (weights / lax.optimization_barrier(jnp.sum(weights, -1, keepdims=True))).astype(jnp.bfloat16)
    mixed = jnp.einsum('hqk,khe->qhe', weights.astype(jnp.float32), value_rows.astype(jnp.float32))
    return mixed.astype(jnp.bfloat16).reshape(queries.shape[0], D)

def reference(hidden, latents_now, latents_next, timestep, version_tags, noise_levels, time_weight, spatial_qkv, spatial_out, temporal_qkv, temporal_out, final_weight):
    table = modulation(timestep, time_weight)
    shift_s = table[0:D]
    scale_s = table[D:2 * D]
    gate_s = table[2 * D:3 * D]
    shift_t = table[3 * D:4 * D]
    scale_t = table[4 * D:5 * D]
    gate_t = table[5 * D:6 * D]
    framed = hidden.reshape(FRAMES, TPF, D)

    def spatial_frame(frame_rows):
        normed = (layer_norm(frame_rows.astype(jnp.float32)) * (1.0 + scale_s) + shift_s).astype(jnp.bfloat16)
        queries, key_rows, value_rows = heads_of(normed, spatial_qkv)
        mixed = attend(queries, key_rows, value_rows)
        projected = jnp.dot(mixed, spatial_out, preferred_element_type=jnp.float32)
        return (frame_rows.astype(jnp.float32) + gate_s * projected).astype(jnp.bfloat16)
    after_spatial = lax.map(spatial_frame, framed)
    columns = jnp.swapaxes(after_spatial, 0, 1)

    def temporal_column(column_rows):
        normed = (layer_norm(column_rows.astype(jnp.float32)) * (1.0 + scale_t) + shift_t).astype(jnp.bfloat16)
        queries, key_rows, value_rows = heads_of(normed, temporal_qkv)
        mixed = attend(queries, key_rows, value_rows)
        return jnp.dot(mixed, temporal_out, preferred_element_type=jnp.float32).astype(jnp.bfloat16)
    temporal_term = jnp.swapaxes(lax.map(temporal_column, columns), 0, 1)
    final_state = after_spatial.astype(jnp.float32) + gate_t * temporal_term.astype(jnp.float32)
    final_normed = layer_norm(final_state).astype(jnp.bfloat16)
    velocity = jnp.einsum('cd,ftd->fct', final_weight.astype(jnp.float32), final_normed.astype(jnp.float32))
    time_value = timestep.astype(jnp.float32)[0] / STEPS
    matches = (version_tags[:, None] == jnp.arange(VERSIONS).astype(jnp.int32)[None, :]).astype(jnp.float32)
    levels = lax.optimization_barrier(jnp.sum(noise_levels[None, :] * matches, 1))
    noise_scale = levels * jnp.sqrt(time_value / (1.0 - time_value))
    factor = (noise_scale * noise_scale / (2.0 * time_value))[:, None, None]
    drift = velocity + factor * (latents_now + (1.0 - time_value) * velocity)
    next_mean = latents_now - drift / STEPS
    spread = noise_scale * math.sqrt(1.0 / STEPS)
    standard = (latents_next - next_mean) / spread[:, None, None]
    log_prob = -0.5 * lax.optimization_barrier(jnp.mean(standard * standard, 1)) - jnp.log(spread)[:, None] - 0.5 * math.log(2.0 * math.pi)
    return (log_prob, next_mean)
```

```python
import math

import jax
import jax.numpy as jnp
from jax import lax
from jax.experimental import pallas as pl
from jax.experimental.pallas import tpu as pltpu
from jax.sharding import PartitionSpec as P

D = 1152
HEADS = 16
HEAD = D // HEADS
C = 16
FREQ = 256
STEPS = 10
VERSIONS = 8
TPF = 256
LANES = 128
CHUNKS = tuple((low, min(512, 3 * D - low)) for low in range(0, 3 * D, 512))
ROWS = 32

norm_eps = 1e-06
f32 = jnp.float32
bf16 = jnp.bfloat16


def iota(shape, dim):
    return lax.broadcasted_iota(jnp.int32, shape, dim)


def centre(values):
    centred = values - jnp.mean(values, -1, keepdims=True)
    variance = jnp.mean(centred * centred, -1, keepdims=True)
    return centred * lax.rsqrt(variance + norm_eps)


def fill_picker(picker):
    for low in range(0, 2 * D, 256):
        column = iota((256, LANES), 0) + low
        lane = iota((256, LANES), 1)
        head = jnp.where(lane < 2 * HEADS, lane, lane - 2 * HEADS)
        offset = column - head * HEAD
        inside = (offset >= 0) & (offset < HEAD) & (lane < 4 * HEADS)
        picker[low : low + 256, :] = jnp.where(inside, 1.0, 0.0).astype(bf16)


def modulate_rows(source, scale, shift, normed):
    def step(index, carry):
        rows = pl.ds(pl.multiple_of(index * ROWS, ROWS), ROWS)
        values = centre(source[rows, :].astype(f32))
        normed[rows, :] = (values * (1.0 + scale) + shift).astype(bf16)
        return carry

    lax.fori_loop(0, TPF // ROWS, step, 0)


def project(normed, weight, picker, raw, packed, ready):
    squares = jnp.zeros((TPF, LANES), f32)
    for index, (low, width) in enumerate(CHUNKS):
        ready(index)
        mixed = jnp.dot(normed[...], weight[:, low : low + width], preferred_element_type=f32)
        part = min(max(2 * D - low, 0), width)
        if part:
            wanted = mixed[:, :part]
            raw[:, low : low + part] = wanted
            squares = squares + jnp.dot(
                (wanted * wanted).astype(bf16),
                picker[low : low + part, :],
                preferred_element_type=f32,
            )
        if part < width:
            packed[:, low + part : low + width] = mixed[:, part:].astype(bf16)
    lane = iota((TPF, LANES), 1)
    head = jnp.where(lane < 2 * HEADS, lane, lane - 2 * HEADS)
    factor = lax.rsqrt(squares * (1.0 / HEAD) + norm_eps)
    factor = factor * jnp.where(head < HEADS, HEAD ** (-0.5) * math.log2(math.e), 1.0)
    coarse = factor.astype(bf16)
    fine = (factor - coarse.astype(f32)).astype(bf16)
    both = jnp.where(lane < 2 * HEADS, coarse.astype(f32), fine.astype(f32)).astype(bf16)
    for low in range(0, 2 * D, 256):
        spread = lax.dot_general(
            both,
            picker[low : low + 256, :],
            (((1,), (1,)), ((), ())),
            preferred_element_type=f32,
        )
        packed[:, low : low + 256] = (raw[:, low : low + 256] * spread).astype(bf16)


def attend(packed, attended, same):
    ones = jnp.ones((TPF, LANES), bf16)
    for head in range(HEADS):
        start = head * HEAD
        low = start // LANES * LANES
        high = -(-(start + HEAD) // LANES) * LANES
        width = high - low
        lane = iota((TPF, width), 1) + low
        inside = (lane >= start) & (lane < start + HEAD)
        queries = packed[:, low:high]
        queries = jnp.where(inside, queries, jnp.zeros_like(queries))
        scores = lax.dot_general(
            queries,
            packed[:, D + low : D + high],
            (((1,), (1,)), ((), ())),
            preferred_element_type=f32,
        )
        weights = jnp.exp2(scores).astype(bf16)
        if same is not None:
            weights = weights * same[...]
        total = jnp.dot(weights, ones, preferred_element_type=f32)
        mixed = jnp.dot(weights, packed[:, 2 * D + low : 2 * D + high], preferred_element_type=f32)
        share = 1.0 / total
        for tile in range(low, high, LANES):
            result = mixed[:, tile - low : tile - low + LANES] * share
            if start > tile:
                keep = iota((TPF, LANES), 1) + tile < start
                result = jnp.where(keep, attended[:, tile : tile + LANES].astype(f32), result)
            attended[:, tile : tile + LANES] = result.astype(bf16)


def spatial_kernel(
    step_ref, hidden_hbm, time_hbm, qkv_hbm, out_hbm,
    after_ref, table_ref,
    hidden, time_weight, qkv, out_weight, picker, normed, raw, packed, attended, sems,
):
    copies = [pltpu.make_async_copy(hidden_hbm, hidden, sems.at[0])]
    copies.append(
        pltpu.make_async_copy(
            time_hbm.at[:, 0 : 2 * D], time_weight.at[:, 0 : 2 * D], sems.at[1]
        )
    )
    for index, (low, width) in enumerate(CHUNKS):
        copies.append(
            pltpu.make_async_copy(
                qkv_hbm.at[:, low : low + width], qkv.at[:, low : low + width], sems.at[2 + index]
            )
        )
    last = 2 + len(CHUNKS)
    copies.append(pltpu.make_async_copy(out_hbm, out_weight, sems.at[last]))
    copies.append(
        pltpu.make_async_copy(
            time_hbm.at[:, 2 * D : 6 * D], time_weight.at[:, 2 * D : 6 * D], sems.at[last + 1]
        )
    )
    for copy in copies:
        copy.start()

    fill_picker(picker)
    time_value = jnp.full((16, FREQ // 2), step_ref[0], jnp.int32).astype(f32) / STEPS
    position = iota((16, FREQ // 2), 1).astype(f32)
    angles = 1000.0 * time_value * jnp.exp(-math.log(10000.0) * position / (FREQ // 2))
    embedded = jnp.concatenate([jnp.cos(angles), jnp.sin(angles)], 1)
    activated = (embedded / (1.0 + jnp.exp(-embedded))).astype(bf16)

    copies[0].wait()
    copies[1].wait()
    first = jnp.dot(activated, time_weight[:, 0 : 2 * D], preferred_element_type=f32)
    modulate_rows(hidden, first[0:1, D : 2 * D], first[0:1, 0:D], normed)
    project(normed, qkv, picker, raw, packed, lambda index: copies[2 + index].wait())
    attend(packed, attended, None)
    copies[last].wait()
    copies[last + 1].wait()
    rest = jnp.dot(activated, time_weight[:, 2 * D : 6 * D], preferred_element_type=f32)
    table_ref[...] = rest[0:8, D:]
    gate = rest[0:1, 0:D]
    for low in range(0, D, 256):
        width = min(256, D - low)
        projected = jnp.dot(
            attended[...], out_weight[:, low : low + width], preferred_element_type=f32
        )
        after_ref[:, low : low + width] = (
            hidden[:, low : low + width].astype(f32) + gate[:, low : low + width] * projected
        ).astype(bf16)


def temporal_kernel(
    after_ref, table_ref, qkv, out_weight, final_weight,
    velocity_ref,
    picker, same, normed, raw, packed, attended, term,
):
    fill_picker(picker)
    parity = (iota((TPF, TPF), 0) ^ iota((TPF, TPF), 1)) & 1
    same[...] = jnp.where(parity == 0, 1.0, 0.0).astype(bf16)
    modulate_rows(after_ref, table_ref[0:1, D : 2 * D], table_ref[0:1, 0:D], normed)
    project(normed, qkv, picker, raw, packed, lambda index: None)
    attend(packed, attended, same)
    for low in range(0, D, 256):
        width = min(256, D - low)
        term[:, low : low + width] = jnp.dot(
            attended[...], out_weight[:, low : low + width], preferred_element_type=f32
        ).astype(bf16)
    gate = table_ref[0:1, 2 * D : 3 * D]

    def step(index, carry):
        rows = pl.ds(pl.multiple_of(index * ROWS, ROWS), ROWS)
        state = after_ref[rows, :].astype(f32) + gate * term[rows, :].astype(f32)
        normed[rows, :] = centre(state).astype(bf16)
        return carry

    lax.fori_loop(0, TPF // ROWS, step, 0)
    velocity_ref[:, 0:C] = lax.dot_general(
        normed[...], final_weight[...], (((1,), (1,)), ((), ())), preferred_element_type=f32
    )
    velocity_ref[:, C:] = jnp.zeros((TPF, LANES - C), f32)


def density_kernel(
    step_ref, tag_ref, level_ref, velocity_ref, now_ref, next_ref, log_ref, mean_ref
):
    velocity = velocity_ref[...].T[0:C, :]
    level = jnp.full((1, TPF), level_ref[tag_ref[0]], f32)
    time_value = jnp.full((1, TPF), step_ref[0], jnp.int32).astype(f32) / STEPS
    noise_scale = level * jnp.sqrt(time_value / (1.0 - time_value))
    factor = noise_scale * noise_scale / (2.0 * time_value)
    now = now_ref[0]
    drift = velocity + factor * (now + (1.0 - time_value) * velocity)
    next_mean = now - drift / STEPS
    spread = noise_scale * math.sqrt(1.0 / STEPS)
    standard = (next_ref[0] - next_mean) / spread
    log_ref[...] = (
        -0.5 * jnp.mean(standard * standard, 0, keepdims=True)
        - jnp.log(spread)
        - 0.5 * math.log(2.0 * math.pi)
    )
    mean_ref[0] = next_mean


ANY = pl.BlockSpec(memory_space=pl.ANY)
VMEM = pl.BlockSpec(memory_space=pltpu.VMEM)
SMEM = pl.BlockSpec(memory_space=pltpu.SMEM)
work = [
    pltpu.VMEM((TPF, D), bf16),
    pltpu.VMEM((TPF, 2 * D), f32),
    pltpu.VMEM((TPF, 3 * D), bf16),
    pltpu.VMEM((TPF, D), bf16),
]


def shards(
    hidden,
    latents_now,
    latents_next,
    timestep,
    version_tags,
    noise_levels,
    time_weight,
    spatial_qkv,
    spatial_out,
    temporal_qkv,
    temporal_out,
    final_weight,
):
    after_spatial, table = pl.pallas_call(
        spatial_kernel,
        out_shape=(
            jax.ShapeDtypeStruct((TPF, D), bf16),
            jax.ShapeDtypeStruct((8, 3 * D), f32),
        ),
        in_specs=[SMEM, ANY, ANY, ANY, ANY],
        out_specs=(VMEM, VMEM),
        scratch_shapes=[
            pltpu.VMEM((TPF, D), bf16),
            pltpu.VMEM((FREQ, 6 * D), bf16),
            pltpu.VMEM((D, 3 * D), bf16),
            pltpu.VMEM((D, D), bf16),
            pltpu.VMEM((2 * D, LANES), bf16),
            *work,
            pltpu.SemaphoreType.DMA((4 + len(CHUNKS),)),
        ],
        compiler_params=pltpu.CompilerParams(vmem_limit_bytes=32 << 20),
        name="spatial",
    )(timestep, hidden, time_weight, spatial_qkv, spatial_out)
    peers = lax.axis_size(("inner", "outer"))
    per_peer = TPF // peers
    blocks = after_spatial.reshape(peers, per_peer, D)
    arrived = lax.all_to_all(blocks, ("inner", "outer"), split_axis=0, concat_axis=0, tiled=True)
    velocity = pl.pallas_call(
        temporal_kernel,
        out_shape=jax.ShapeDtypeStruct((TPF, LANES), f32),
        in_specs=[VMEM] * 5,
        out_specs=VMEM,
        scratch_shapes=[
            pltpu.VMEM((2 * D, LANES), bf16),
            pltpu.VMEM((TPF, TPF), bf16),
            *work,
            pltpu.VMEM((TPF, D), bf16),
        ],
        compiler_params=pltpu.CompilerParams(vmem_limit_bytes=32 << 20),
        name="temporal",
    )(arrived.reshape(TPF, D), table, temporal_qkv, temporal_out, final_weight)
    returned = lax.all_to_all(
        velocity.reshape(peers, per_peer, LANES),
        ("inner", "outer"),
        split_axis=0,
        concat_axis=0,
        tiled=True,
    )
    return pl.pallas_call(
        density_kernel,
        out_shape=(
            jax.ShapeDtypeStruct((1, TPF), f32),
            jax.ShapeDtypeStruct((1, C, TPF), f32),
        ),
        in_specs=[SMEM, SMEM, SMEM, VMEM, VMEM, VMEM],
        out_specs=(VMEM, VMEM),
        name="density",
    )(
        timestep, version_tags, noise_levels, returned.reshape(TPF, LANES), latents_now, latents_next
    )


def solution(mesh):
    return jax.shard_map(
        shards,
        mesh=mesh,
        in_specs=(
            P(("inner", "outer"), None),
            P(("inner", "outer"), None, None),
            P(("inner", "outer"), None, None),
            P(),
            P(("inner", "outer")),
            P(),
            P(),
            P(),
            P(),
            P(),
            P(),
            P(),
        ),
        out_specs=(P(("inner", "outer"), None), P(("inner", "outer"), None, None)),
        check_vma=False,
    )
```

```python
import math

import jax
import jax.numpy as jnp
from jax import lax
from jax.experimental import pallas as pl
from jax.experimental.pallas import tpu as pltpu
from jax.sharding import PartitionSpec as P

D = 1152
HEADS = 16
HEAD = D // HEADS
C = 16
FREQ = 256
STEPS = 10
VERSIONS = 8
TPF = 256
LANES = 128
CHUNKS = tuple((low, min(512, 3 * D - low)) for low in range(0, 3 * D, 512))
OUT_CHUNKS = tuple((low, min(512, D - low)) for low in range(0, D, 512))
ROWS = 32
SPATIAL_VMEM = 40 << 20
PREPARE_VMEM = 8 << 20

norm_eps = 1e-06
f32 = jnp.float32
bf16 = jnp.bfloat16


def iota(shape, dim):
    return lax.broadcasted_iota(jnp.int32, shape, dim)


def centre(values):
    centred = values - jnp.mean(values, -1, keepdims=True)
    variance = jnp.mean(centred * centred, -1, keepdims=True)
    return centred * lax.rsqrt(variance + norm_eps)


def fill_picker(picker):
    for low in range(0, 2 * D, 256):
        column = iota((256, LANES), 0) + low
        lane = iota((256, LANES), 1)
        head = jnp.where(lane < 2 * HEADS, lane, lane - 2 * HEADS)
        offset = column - head * HEAD
        inside = (offset >= 0) & (offset < HEAD) & (lane < 4 * HEADS)
        picker[low : low + 256, :] = jnp.where(inside, 1.0, 0.0).astype(bf16)


def modulate_rows(source, scale, shift, normed):
    def step(index, carry):
        rows = pl.ds(pl.multiple_of(index * ROWS, ROWS), ROWS)
        values = centre(source[rows, :].astype(f32))
        normed[rows, :] = (values * (1.0 + scale) + shift).astype(bf16)
        return carry

    lax.fori_loop(0, TPF // ROWS, step, 0, unroll=True)


def project(normed, weight, picker, raw, packed, ready):
    squares = jnp.zeros((TPF, LANES), f32)
    for index, (low, width) in enumerate(CHUNKS):
        ready(index)
        mixed = jnp.dot(normed[...], weight[:, low : low + width], preferred_element_type=f32)
        part = min(max(2 * D - low, 0), width)
        if part:
            wanted = mixed[:, :part]
            raw[:, low : low + part] = wanted
            squares = squares + jnp.dot(
                (wanted * wanted).astype(bf16),
                picker[low : low + part, :],
                preferred_element_type=f32,
            )
        if part < width:
            packed[:, low + part : low + width] = mixed[:, part:].astype(bf16)
    lane = iota((TPF, LANES), 1)
    head = jnp.where(lane < 2 * HEADS, lane, lane - 2 * HEADS)
    factor = lax.rsqrt(squares * (1.0 / HEAD) + norm_eps)
    factor = factor * jnp.where(head < HEADS, HEAD ** (-0.5) * math.log2(math.e), 1.0)
    coarse = factor.astype(bf16)
    fine = (factor - coarse.astype(f32)).astype(bf16)
    both = jnp.where(lane < 2 * HEADS, coarse.astype(f32), fine.astype(f32)).astype(bf16)
    for low in range(0, 2 * D, 256):
        spread = lax.dot_general(
            both,
            picker[low : low + 256, :],
            (((1,), (1,)), ((), ())),
            preferred_element_type=f32,
        )
        packed[:, low : low + 256] = (raw[:, low : low + 256] * spread).astype(bf16)


def attend(packed, attended, same):
    ones = jnp.ones((TPF, LANES), bf16)
    lane = iota((TPF, LANES), 1)
    pending = None
    for head in range(HEADS):
        start = head * HEAD
        low = start // LANES * LANES
        high = -(-(start + HEAD) // LANES) * LANES
        wide = iota((TPF, high - low), 1) + low
        inside = (wide >= start) & (wide < start + HEAD)
        queries = packed[:, low:high]
        scores = lax.dot_general(
            jnp.where(inside, queries, jnp.zeros_like(queries)),
            packed[:, D + low : D + high],
            (((1,), (1,)), ((), ())),
            preferred_element_type=f32,
        )
        weights = jnp.exp2(scores).astype(bf16)
        if same is not None:
            weights = weights * same[...]
        values = packed[:, 2 * D + low : 2 * D + high]
        single = high - low == LANES
        if single:
            values = jnp.concatenate([values, ones], 1)
        else:
            values = jnp.where(inside, values, jnp.ones_like(values))
        mixed = jnp.dot(weights, values, preferred_element_type=f32)
        left, right = mixed[:, :LANES], mixed[:, LANES:]
        before = lane < start - low
        share = 1.0 / (right if single else jnp.where(before, left, right))
        left = left * share
        if start > low:
            left = jnp.where(before, pending, left)
        pending = left if single else right * share
        if start + HEAD >= low + LANES:
            attended[:, low : low + LANES] = left.astype(bf16)


def embed(step_ref):
    time_value = jnp.full((16, FREQ // 2), step_ref[0], jnp.int32).astype(f32) / STEPS
    position = iota((16, FREQ // 2), 1).astype(f32)
    angles = 1000.0 * time_value * jnp.exp(-math.log(10000.0) * position / (FREQ // 2))
    embedded = jnp.concatenate([jnp.cos(angles), jnp.sin(angles)], 1)
    return (embedded / (1.0 + jnp.exp(-embedded))).astype(bf16)


def spatial_kernel(
    step_ref, hidden_hbm, time_hbm, qkv_hbm, out_hbm,
    after_ref,
    hidden, time_weight, qkv, out_weight, picker, normed, raw, packed, attended, sems,
):
    copies = [pltpu.make_async_copy(hidden_hbm, hidden, sems.at[0])]
    copies.append(
        pltpu.make_async_copy(
            time_hbm.at[:, 0 : 2 * D], time_weight.at[:, 0 : 2 * D], sems.at[1]
        )
    )
    for index, (low, width) in enumerate(CHUNKS):
        copies.append(
            pltpu.make_async_copy(
                qkv_hbm.at[:, low : low + width], qkv.at[:, low : low + width], sems.at[2 + index]
            )
        )
    last = 2 + len(CHUNKS)
    copies.append(
        pltpu.make_async_copy(
            time_hbm.at[:, 2 * D : 3 * D], time_weight.at[:, 2 * D : 3 * D], sems.at[last]
        )
    )
    copies.append(pltpu.make_async_copy(out_hbm, out_weight, sems.at[last + 1]))
    for copy in copies:
        copy.start()

    fill_picker(picker)
    activated = embed(step_ref)
    copies[0].wait()
    copies[1].wait()
    first = jnp.dot(activated, time_weight[:, 0 : 2 * D], preferred_element_type=f32)
    modulate_rows(hidden, first[0:1, D : 2 * D], first[0:1, 0:D], normed)
    project(normed, qkv, picker, raw, packed, lambda index: copies[2 + index].wait())
    attend(packed, attended, None)
    copies[last].wait()
    gate = jnp.dot(activated, time_weight[:, 2 * D : 3 * D], preferred_element_type=f32)[0:1, :]
    copies[last + 1].wait()
    for low, width in OUT_CHUNKS:
        projected = jnp.dot(
            attended[...], out_weight[:, low : low + width], preferred_element_type=f32
        )
        after = hidden[:, low : low + width].astype(f32) + gate[:, low : low + width] * projected
        after_ref[:, :, low : low + width] = after.astype(bf16).reshape(TPF // 2, 2, width)


def prepare_kernel(
    step_ref, time_hbm, table_hbm, picker_hbm, same_hbm, time_weight, table, picker, same, sems
):
    copy = pltpu.make_async_copy(time_hbm.at[:, 3 * D : 6 * D], time_weight, sems.at[0])
    copy.start()
    fill_picker(picker)
    parity = (iota((TPF, TPF), 0) ^ iota((TPF, TPF), 1)) & 1
    same[...] = jnp.where(parity == 0, 1.0, 0.0).astype(bf16)
    activated = embed(step_ref)
    copy.wait()
    table[...] = jnp.dot(activated, time_weight[...], preferred_element_type=f32)[0:8]
    copies = [
        pltpu.make_async_copy(source, target, sems.at[1 + index])
        for index, (source, target) in enumerate(
            ((table, table_hbm), (picker, picker_hbm), (same, same_hbm))
        )
    ]
    for copy in copies:
        copy.start()
    for copy in copies:
        copy.wait()


def temporal_kernel(
    arrived_ref, table_hbm, picker_hbm, same_hbm, qkv_hbm, out_hbm, final_hbm,
    velocity_ref,
    table, picker, same, qkv, out_weight, final_weight,
    normed, raw, packed, attended, term, after, sems,
):
    pairs = [(table_hbm, table), (picker_hbm, picker)]
    for low, width in CHUNKS:
        pairs.append((qkv_hbm.at[:, low : low + width], qkv.at[:, low : low + width]))
    last = len(pairs)
    pairs += [(same_hbm, same), (out_hbm, out_weight), (final_hbm, final_weight)]
    copies = [
        pltpu.make_async_copy(source, target, sems.at[index])
        for index, (source, target) in enumerate(pairs)
    ]
    for copy in copies:
        copy.start()

    after[...] = arrived_ref[...].reshape(TPF, D)
    copies[0].wait()
    modulate_rows(after, table[0:1, D : 2 * D], table[0:1, 0:D], normed)
    copies[1].wait()
    project(normed, qkv, picker, raw, packed, lambda index: copies[2 + index].wait())
    copies[last].wait()
    attend(packed, attended, same)
    copies[last + 1].wait()
    for low, width in OUT_CHUNKS:
        term[:, low : low + width] = jnp.dot(
            attended[...], out_weight[:, low : low + width], preferred_element_type=f32
        ).astype(bf16)
    gate = table[0:1, 2 * D : 3 * D]

    def step(index, carry):
        rows = pl.ds(pl.multiple_of(index * ROWS, ROWS), ROWS)
        state = after[rows, :].astype(f32) + gate * term[rows, :].astype(f32)
        normed[rows, :] = centre(state).astype(bf16)
        return carry

    lax.fori_loop(0, TPF // ROWS, step, 0, unroll=True)
    copies[last + 2].wait()
    velocity_ref[:, 0:C] = lax.dot_general(
        normed[...], final_weight[...], (((1,), (1,)), ((), ())), preferred_element_type=f32
    )
    velocity_ref[:, C:] = jnp.zeros((TPF, LANES - C), f32)


def density_kernel(
    step_ref, tag_ref, level_ref, velocity_ref, now_ref, next_ref, log_ref, mean_ref
):
    velocity = velocity_ref[...].T[0:C, :]
    level = jnp.full((1, TPF), level_ref[tag_ref[0]], f32)
    time_value = jnp.full((1, TPF), step_ref[0], jnp.int32).astype(f32) / STEPS
    noise_scale = level * jnp.sqrt(time_value / (1.0 - time_value))
    factor = noise_scale * noise_scale / (2.0 * time_value)
    now = now_ref[0]
    drift = velocity + factor * (now + (1.0 - time_value) * velocity)
    next_mean = now - drift / STEPS
    spread = noise_scale * math.sqrt(1.0 / STEPS)
    standard = (next_ref[0] - next_mean) / spread
    log_ref[...] = (
        -0.5 * jnp.mean(standard * standard, 0, keepdims=True)
        - jnp.log(spread)
        - 0.5 * math.log(2.0 * math.pi)
    )
    mean_ref[0] = next_mean


HBM = pl.BlockSpec(memory_space=pltpu.HBM)
VMEM = pl.BlockSpec(memory_space=pltpu.VMEM)
SMEM = pl.BlockSpec(memory_space=pltpu.SMEM)
work = [
    pltpu.VMEM((TPF, D), bf16),
    pltpu.VMEM((TPF, 2 * D), f32),
    pltpu.VMEM((TPF, 3 * D), bf16),
    pltpu.VMEM((TPF, D), bf16),
]


def in_hbm(array):
    return pltpu.with_memory_space_constraint(array, pltpu.HBM)


def shards(
    hidden,
    latents_now,
    latents_next,
    timestep,
    version_tags,
    noise_levels,
    time_weight,
    spatial_qkv,
    spatial_out,
    temporal_qkv,
    temporal_out,
    final_weight,
):
    time_weight = in_hbm(time_weight)
    after_spatial = pl.pallas_call(
        spatial_kernel,
        out_shape=jax.ShapeDtypeStruct((TPF // 2, 2, D), bf16),
        in_specs=[SMEM, HBM, HBM, HBM, HBM],
        out_specs=VMEM,
        scratch_shapes=[
            pltpu.VMEM((TPF, D), bf16),
            pltpu.VMEM((FREQ, 3 * D), bf16),
            pltpu.VMEM((D, 3 * D), bf16),
            pltpu.VMEM((D, D), bf16),
            pltpu.VMEM((2 * D, LANES), bf16),
            *work,
            pltpu.SemaphoreType.DMA((4 + len(CHUNKS),)),
        ],
        compiler_params=pltpu.CompilerParams(vmem_limit_bytes=SPATIAL_VMEM),
        cost_estimate=pl.CostEstimate(
            flops=4 << 30, bytes_accessed=14 << 20, transcendentals=1 << 20
        ),
        name="spatial",
    )(timestep, in_hbm(hidden), time_weight, in_hbm(spatial_qkv), in_hbm(spatial_out))
    arrived = lax.all_to_all(
        after_spatial, ("inner", "outer"), split_axis=0, concat_axis=0, tiled=True
    )
    table, picker, same = pl.pallas_call(
        prepare_kernel,
        out_shape=(
            jax.ShapeDtypeStruct((8, 3 * D), f32),
            jax.ShapeDtypeStruct((2 * D, LANES), bf16),
            jax.ShapeDtypeStruct((TPF, TPF), bf16),
        ),
        in_specs=[SMEM, HBM],
        out_specs=(HBM, HBM, HBM),
        scratch_shapes=[
            pltpu.VMEM((FREQ, 3 * D), bf16),
            pltpu.VMEM((8, 3 * D), f32),
            pltpu.VMEM((2 * D, LANES), bf16),
            pltpu.VMEM((TPF, TPF), bf16),
            pltpu.SemaphoreType.DMA((4,)),
        ],
        compiler_params=pltpu.CompilerParams(vmem_limit_bytes=PREPARE_VMEM),
        cost_estimate=pl.CostEstimate(
            flops=32 << 20, bytes_accessed=3 << 20, transcendentals=1 << 13
        ),
        name="prepare",
    )(timestep, time_weight)
    velocity = pl.pallas_call(
        temporal_kernel,
        out_shape=jax.ShapeDtypeStruct((TPF, LANES), f32),
        in_specs=[VMEM] + [HBM] * 6,
        out_specs=VMEM,
        scratch_shapes=[
            pltpu.VMEM((8, 3 * D), f32),
            pltpu.VMEM((2 * D, LANES), bf16),
            pltpu.VMEM((TPF, TPF), bf16),
            pltpu.VMEM((D, 3 * D), bf16),
            pltpu.VMEM((D, D), bf16),
            pltpu.VMEM((C, D), bf16),
            *work,
            pltpu.VMEM((TPF, D), bf16),
            pltpu.VMEM((TPF, D), bf16),
            pltpu.SemaphoreType.DMA((5 + len(CHUNKS),)),
        ],
        compiler_params=pltpu.CompilerParams(vmem_limit_bytes=40 << 20),
        cost_estimate=pl.CostEstimate(
            flops=4 << 30, bytes_accessed=12 << 20, transcendentals=1 << 20
        ),
        name="temporal",
    )(
        arrived,
        table,
        picker,
        same,
        in_hbm(temporal_qkv),
        in_hbm(temporal_out),
        in_hbm(final_weight),
    )
    returned = lax.all_to_all(
        velocity.reshape(TPF // 2, 2, LANES),
        ("inner", "outer"),
        split_axis=0,
        concat_axis=0,
        tiled=True,
    )
    return pl.pallas_call(
        density_kernel,
        out_shape=(
            jax.ShapeDtypeStruct((1, TPF), f32),
            jax.ShapeDtypeStruct((1, C, TPF), f32),
        ),
        in_specs=[SMEM, SMEM, SMEM, VMEM, VMEM, VMEM],
        out_specs=(VMEM, VMEM),
        compiler_params=pltpu.CompilerParams(vmem_limit_bytes=4 << 20),
        name="density",
    )(
        timestep, version_tags, noise_levels, returned.reshape(TPF, LANES), latents_now, latents_next
    )


def solution(mesh):
    return jax.shard_map(
        shards,
        mesh=mesh,
        in_specs=(
            P(("inner", "outer"), None),
            P(("inner", "outer"), None, None),
            P(("inner", "outer"), None, None),
            P(),
            P(("inner", "outer")),
            P(),
            P(),
            P(),
            P(),
            P(),
            P(),
            P(),
        ),
        out_specs=(P(("inner", "outer"), None), P(("inner", "outer"), None, None)),
        check_vma=False,
    )
```

```python
import math

import jax
import jax.numpy as jnp
from jax import lax
from jax.experimental import pallas as pl
from jax.experimental.pallas import tpu as pltpu
from jax.sharding import PartitionSpec as P

D = 1152
HEADS = 16
HEAD = D // HEADS
C = 16
FREQ = 256
STEPS = 10
VERSIONS = 8
TPF = 256
LANES = 128
OUT_CHUNKS = tuple((low, min(512, D - low)) for low in range(0, D, 512))
ROWS = 32

norm_eps = 1e-06
f32 = jnp.float32
bf16 = jnp.bfloat16


def iota(shape, dim):
    return lax.broadcasted_iota(jnp.int32, shape, dim)


def centre(values):
    centred = values - jnp.mean(values, -1, keepdims=True)
    variance = jnp.mean(centred * centred, -1, keepdims=True)
    return centred * lax.rsqrt(variance + norm_eps)


def fill_picker(picker):
    for low in range(0, 2 * D, 256):
        column = iota((256, LANES), 0) + low
        lane = iota((256, LANES), 1)
        head = jnp.where(lane < 2 * HEADS, lane, lane - 2 * HEADS)
        offset = column - head * HEAD
        inside = (offset >= 0) & (offset < HEAD) & (lane < 4 * HEADS)
        picker[low : low + 256, :] = jnp.where(inside, 1.0, 0.0).astype(bf16)


def by_rows(step):
    def one(index, carry):
        step(pl.ds(pl.multiple_of(index * ROWS, ROWS), ROWS))
        return carry

    lax.fori_loop(0, TPF // ROWS, one, 0, unroll=True)


def embed(step_ref):
    time_value = jnp.full((16, FREQ // 2), step_ref[0], jnp.int32).astype(f32) / STEPS
    position = iota((16, FREQ // 2), 1).astype(f32)
    angles = 1000.0 * time_value * jnp.exp(-math.log(10000.0) * position / (FREQ // 2))
    embedded = jnp.concatenate([jnp.cos(angles), jnp.sin(angles)], 1)
    return (embedded / (1.0 + jnp.exp(-embedded))).astype(bf16)


def copies_of(pairs, sems):
    copies = [
        pltpu.make_async_copy(source, target, sems.at[index])
        for index, (source, target) in enumerate(pairs)
    ]
    for copy in copies:
        copy.start()
    return copies


def project(normed, weights, picker, raw, packed, ready):
    def product(part):
        ready(part)
        return jnp.dot(normed[...], weights[part][...], preferred_element_type=f32)

    def square_sums(part):
        total = jnp.zeros((TPF, LANES), f32)
        for low, width in OUT_CHUNKS:
            span = slice(part * D + low, part * D + low + width)
            values = raw[:, span]
            total = total + jnp.dot(
                (values * values).astype(bf16), picker[span, :], preferred_element_type=f32
            )
        return total

    raw[:, 0:D] = product(0)
    raw[:, D : 2 * D] = product(1)
    squares = square_sums(0)
    packed[:, 2 * D : 3 * D] = product(2).astype(bf16)
    squares = squares + square_sums(1)
    lane = iota((TPF, LANES), 1)
    head = jnp.where(lane < 2 * HEADS, lane, lane - 2 * HEADS)
    factor = lax.rsqrt(squares * (1.0 / HEAD) + norm_eps)
    factor = factor * jnp.where(head < HEADS, HEAD ** (-0.5) * math.log2(math.e), 1.0)
    coarse = factor.astype(bf16)
    fine = (factor - coarse.astype(f32)).astype(bf16)
    both = jnp.where(lane < 2 * HEADS, coarse.astype(f32), fine.astype(f32)).astype(bf16)
    for low in range(0, 2 * D, 256):
        spread = lax.dot_general(
            both,
            picker[low : low + 256, :],
            (((1,), (1,)), ((), ())),
            preferred_element_type=f32,
        )
        packed[:, low : low + 256] = (raw[:, low : low + 256] * spread).astype(bf16)


def attend(packed, attended, same):
    ones = jnp.ones((TPF, LANES), bf16)
    lane = iota((TPF, LANES), 1)
    pending = None
    for head in range(HEADS):
        start = head * HEAD
        low = start // LANES * LANES
        high = -(-(start + HEAD) // LANES) * LANES
        wide = iota((TPF, high - low), 1) + low
        inside = (wide >= start) & (wide < start + HEAD)
        queries = packed[:, low:high]
        scores = lax.dot_general(
            jnp.where(inside, queries, jnp.zeros_like(queries)),
            packed[:, D + low : D + high],
            (((1,), (1,)), ((), ())),
            preferred_element_type=f32,
        )
        weights = jnp.exp2(scores).astype(bf16)
        if same is not None:
            weights = weights * same[...]
        values = packed[:, 2 * D + low : 2 * D + high]
        single = high - low == LANES
        if single:
            values = jnp.concatenate([values, ones], 1)
        else:
            values = jnp.where(inside, values, jnp.ones_like(values))
        mixed = jnp.dot(weights, values, preferred_element_type=f32)
        left, right = mixed[:, :LANES], mixed[:, LANES:]
        before = lane < start - low
        share = 1.0 / (right if single else jnp.where(before, left, right))
        left = left * share
        if start > low:
            left = jnp.where(before, pending, left)
        pending = left if single else right * share
        if start + HEAD >= low + LANES:
            attended[:, low : low + LANES] = left.astype(bf16)


def spatial_kernel(
    step_ref, hidden_hbm, time_hbm, qkv_hbm, out_hbm,
    after_ref,
    hidden, modulation, gate_weight, query, key, value, out_weight, picker, normed, raw,
    packed, attended, sems,
):
    parts = (query, key, value)
    pairs = [(hidden_hbm, hidden), (time_hbm.at[:, 0 : 2 * D], modulation)]
    pairs += [(qkv_hbm.at[:, part * D : (part + 1) * D], parts[part]) for part in range(3)]
    pairs += [(time_hbm.at[:, 2 * D : 3 * D], gate_weight), (out_hbm, out_weight)]
    copies = copies_of(pairs, sems)

    fill_picker(picker)
    activated = embed(step_ref)
    copies[0].wait()

    def normalise(rows):
        raw[rows, 0:D] = centre(hidden[rows, :].astype(f32))

    by_rows(normalise)
    copies[1].wait()
    table = jnp.dot(activated, modulation[...], preferred_element_type=f32)
    shift, scale = table[0:1, 0:D], 1.0 + table[0:1, D : 2 * D]

    def modulate(rows):
        normed[rows, :] = (raw[rows, 0:D] * scale + shift).astype(bf16)

    by_rows(modulate)
    project(normed, parts, picker, raw, packed, lambda part: copies[2 + part].wait())
    attend(packed, attended, None)
    copies[5].wait()
    copies[6].wait()
    gate = jnp.dot(activated, gate_weight[...], preferred_element_type=f32)[0:1, :]
    for low, width in OUT_CHUNKS:
        projected = jnp.dot(
            attended[...], out_weight[:, low : low + width], preferred_element_type=f32
        )
        after = hidden[:, low : low + width].astype(f32) + gate[:, low : low + width] * projected
        after_ref[:, :, low : low + width] = after.astype(bf16).reshape(TPF // 2, 2, width)


def prepare_kernel(
    step_ref, tag_ref, level_ref, time_hbm, qkv_hbm,
    table_hbm, query_hbm, terms_hbm,
    modulation, table, terms, sems,
):
    copies = copies_of(
        [
            (time_hbm.at[:, 3 * D : 6 * D], modulation),
            (qkv_hbm.at[:, 0:D], query_hbm),
        ],
        sems,
    )
    activated = embed(step_ref)
    level = jnp.full((8, LANES), level_ref[tag_ref[0]], f32)
    time_value = jnp.full((8, LANES), step_ref[0], jnp.int32).astype(f32) / STEPS
    noise_scale = level * jnp.sqrt(time_value / (1.0 - time_value))
    spread = noise_scale * math.sqrt(1.0 / STEPS)
    terms[0:8, :] = noise_scale * noise_scale / (2.0 * time_value)
    terms[8:16, :] = 1.0 - time_value
    terms[16:24, :] = spread
    terms[24:32, :] = -jnp.log(spread)
    copies[0].wait()
    table[...] = jnp.dot(activated, modulation[...], preferred_element_type=f32)[0:8]
    results = [
        pltpu.make_async_copy(table, table_hbm, sems.at[2]),
        pltpu.make_async_copy(terms, terms_hbm, sems.at[3]),
    ]
    for copy in results:
        copy.start()
    for copy in results:
        copy.wait()
    copies[1].wait()


def temporal_kernel(
    arrived_ref, table, query, qkv_hbm, out_hbm, final_hbm,
    velocity_ref,
    picker, same, key, value, out_weight, final_weight,
    normed, raw, packed, attended, term, after, sems,
):
    copies = copies_of(
        [
            (qkv_hbm.at[:, D : 2 * D], key),
            (qkv_hbm.at[:, 2 * D : 3 * D], value),
            (out_hbm, out_weight),
            (final_hbm, final_weight),
        ],
        sems,
    )
    after[...] = arrived_ref[...].reshape(TPF, D)
    fill_picker(picker)
    parity = (iota((TPF, TPF), 0) ^ iota((TPF, TPF), 1)) & 1
    same[...] = jnp.where(parity == 0, 1.0, 0.0).astype(bf16)
    shift, scale = table[0:1, 0:D], 1.0 + table[0:1, D : 2 * D]
    gate = table[0:1, 2 * D : 3 * D]

    def modulate(rows):
        normed[rows, :] = (centre(after[rows, :].astype(f32)) * scale + shift).astype(bf16)

    by_rows(modulate)

    def ready(part):
        if part:
            copies[part - 1].wait()

    project(normed, (query, key, value), picker, raw, packed, ready)
    attend(packed, attended, same)
    copies[2].wait()
    copies[3].wait()
    for low, width in OUT_CHUNKS:
        term[:, low : low + width] = jnp.dot(
            attended[...], out_weight[:, low : low + width], preferred_element_type=f32
        ).astype(bf16)

    def finish(rows):
        state = after[rows, :].astype(f32) + gate * term[rows, :].astype(f32)
        normed[rows, :] = centre(state).astype(bf16)

    by_rows(finish)
    velocity_ref[:, 0:C] = lax.dot_general(
        normed[...], final_weight[...], (((1,), (1,)), ((), ())), preferred_element_type=f32
    )
    velocity_ref[:, C:] = jnp.zeros((TPF, LANES - C), f32)


def density_kernel(terms_ref, velocity_ref, now_ref, next_ref, log_ref, mean_ref):
    velocity = velocity_ref[...].T[0:C, :]
    factor, rest, spread, minus_log = (terms_ref[8 * row : 8 * row + 1, 0:1] for row in range(4))
    now = now_ref[0]
    drift = velocity + factor * (now + rest * velocity)
    next_mean = now - drift / STEPS
    standard = (next_ref[0] - next_mean) / spread
    log_ref[...] = (
        -0.5 * jnp.mean(standard * standard, 0, keepdims=True)
        + minus_log
        - 0.5 * math.log(2.0 * math.pi)
    )
    mean_ref[0] = next_mean


SMEM = pl.BlockSpec(memory_space=pltpu.SMEM)
HBM = pl.BlockSpec(memory_space=pltpu.HBM)
VMEM = pl.BlockSpec(memory_space=pltpu.VMEM)
work = [
    pltpu.VMEM((TPF, D), bf16),
    pltpu.VMEM((TPF, 2 * D), f32),
    pltpu.VMEM((TPF, 3 * D), bf16),
    pltpu.VMEM((TPF, D), bf16),
]


def in_hbm(array):
    return pltpu.with_memory_space_constraint(array, pltpu.HBM)


def shards(
    hidden,
    latents_now,
    latents_next,
    timestep,
    version_tags,
    noise_levels,
    time_weight,
    spatial_qkv,
    spatial_out,
    temporal_qkv,
    temporal_out,
    final_weight,
):
    time_weight, temporal_qkv = in_hbm(time_weight), in_hbm(temporal_qkv)
    part = pltpu.VMEM((D, D), bf16)
    picker = pltpu.VMEM((2 * D, LANES), bf16)
    after_spatial = pl.pallas_call(
        spatial_kernel,
        out_shape=jax.ShapeDtypeStruct((TPF // 2, 2, D), bf16),
        in_specs=[SMEM] + [HBM] * 4,
        out_specs=VMEM,
        scratch_shapes=[
            pltpu.VMEM((TPF, D), bf16),
            pltpu.VMEM((FREQ, 2 * D), bf16),
            pltpu.VMEM((FREQ, D), bf16),
            part,
            part,
            part,
            part,
            picker,
            *work,
            pltpu.SemaphoreType.DMA((7,)),
        ],
        compiler_params=pltpu.CompilerParams(vmem_limit_bytes=40 << 20),
        cost_estimate=pl.CostEstimate(
            flops=4 << 30, bytes_accessed=14 << 20, transcendentals=1 << 20
        ),
        name="spatial",
    )(timestep, in_hbm(hidden), time_weight, in_hbm(spatial_qkv), in_hbm(spatial_out))
    arrived = lax.all_to_all(
        after_spatial, ("inner", "outer"), split_axis=0, concat_axis=0, tiled=True
    )
    table, query, terms = pl.pallas_call(
        prepare_kernel,
        out_shape=(
            jax.ShapeDtypeStruct((8, 3 * D), f32),
            jax.ShapeDtypeStruct((D, D), bf16),
            jax.ShapeDtypeStruct((32, LANES), f32),
        ),
        in_specs=[SMEM] * 3 + [HBM] * 2,
        out_specs=(HBM, HBM, HBM),
        scratch_shapes=[
            pltpu.VMEM((FREQ, 3 * D), bf16),
            pltpu.VMEM((8, 3 * D), f32),
            pltpu.VMEM((32, LANES), f32),
            pltpu.SemaphoreType.DMA((4,)),
        ],
        compiler_params=pltpu.CompilerParams(vmem_limit_bytes=8 << 20),
        cost_estimate=pl.CostEstimate(
            flops=32 << 20, bytes_accessed=8 << 20, transcendentals=1 << 13
        ),
        name="prepare",
    )(timestep, version_tags, noise_levels, time_weight, temporal_qkv)
    velocity = pl.pallas_call(
        temporal_kernel,
        out_shape=jax.ShapeDtypeStruct((TPF, LANES), f32),
        in_specs=[VMEM] * 3 + [HBM] * 3,
        out_specs=VMEM,
        scratch_shapes=[
            picker,
            pltpu.VMEM((TPF, TPF), bf16),
            part,
            part,
            part,
            pltpu.VMEM((C, D), bf16),
            *work,
            pltpu.VMEM((TPF, D), bf16),
            pltpu.VMEM((TPF, D), bf16),
            pltpu.SemaphoreType.DMA((4,)),
        ],
        compiler_params=pltpu.CompilerParams(vmem_limit_bytes=40 << 20),
        cost_estimate=pl.CostEstimate(
            flops=4 << 30, bytes_accessed=12 << 20, transcendentals=1 << 20
        ),
        name="temporal",
    )(arrived, table, query, temporal_qkv, in_hbm(temporal_out), in_hbm(final_weight))
    returned = lax.all_to_all(
        velocity.reshape(TPF // 2, 2, LANES),
        ("inner", "outer"),
        split_axis=0,
        concat_axis=0,
        tiled=True,
    )
    return pl.pallas_call(
        density_kernel,
        out_shape=(
            jax.ShapeDtypeStruct((1, TPF), f32),
            jax.ShapeDtypeStruct((1, C, TPF), f32),
        ),
        in_specs=[VMEM] * 4,
        out_specs=(VMEM, VMEM),
        compiler_params=pltpu.CompilerParams(vmem_limit_bytes=4 << 20),
        name="density",
    )(terms, returned.reshape(TPF, LANES), latents_now, latents_next)


def solution(mesh):
    return jax.shard_map(
        shards,
        mesh=mesh,
        in_specs=(
            P(("inner", "outer"), None),
            P(("inner", "outer"), None, None),
            P(("inner", "outer"), None, None),
            P(),
            P(("inner", "outer")),
            P(),
            P(),
            P(),
            P(),
            P(),
            P(),
            P(),
        ),
        out_specs=(P(("inner", "outer"), None), P(("inner", "outer"), None, None)),
        check_vma=False,
    )
```

```python
import math

import jax
import jax.numpy as jnp
from jax import lax
from jax.experimental import pallas as pl
from jax.experimental.pallas import tpu as pltpu
from jax.sharding import PartitionSpec as P

D = 1152
HEADS = 16
HEAD = D // HEADS
C = 16
FREQ = 256
STEPS = 10
VERSIONS = 8
TPF = 256
LANES = 128
OUT_CHUNKS = tuple((low, min(512, D - low)) for low in range(0, D, 512))
FIRST = 512
ROWS = 32

norm_eps = 1e-06
f32 = jnp.float32
bf16 = jnp.bfloat16


def iota(shape, dim):
    return lax.broadcasted_iota(jnp.int32, shape, dim)


def centre(values):
    centred = values - jnp.mean(values, -1, keepdims=True)
    variance = jnp.mean(centred * centred, -1, keepdims=True)
    return centred * lax.rsqrt(variance + norm_eps)


def fill_picker(picker):
    for low in range(0, 2 * D, 256):
        column = iota((256, LANES), 0) + low
        lane = iota((256, LANES), 1)
        head = jnp.where(lane < 2 * HEADS, lane, lane - 2 * HEADS)
        offset = column - head * HEAD
        inside = (offset >= 0) & (offset < HEAD) & (lane < 4 * HEADS)
        picker[low : low + 256, :] = jnp.where(inside, 1.0, 0.0).astype(bf16)


def by_rows(step):
    def one(index, carry):
        step(pl.ds(pl.multiple_of(index * ROWS, ROWS), ROWS))
        return carry

    lax.fori_loop(0, TPF // ROWS, one, 0, unroll=True)


def embed(step_ref):
    time_value = jnp.full((16, FREQ // 2), step_ref[0], jnp.int32).astype(f32) / STEPS
    position = iota((16, FREQ // 2), 1).astype(f32)
    angles = 1000.0 * time_value * jnp.exp(-math.log(10000.0) * position / (FREQ // 2))
    embedded = jnp.concatenate([jnp.cos(angles), jnp.sin(angles)], 1)
    return (embedded / (1.0 + jnp.exp(-embedded))).astype(bf16)


def copies_of(pairs, sems):
    copies = [
        pltpu.make_async_copy(source, target, sems.at[index])
        for index, (source, target) in enumerate(pairs)
    ]
    for copy in copies:
        copy.start()
    return copies


def project(normed, weights, picker, raw, packed, ready, first):
    def product(part, low=0, high=D):
        return jnp.dot(normed[...], weights[part][:, low:high], preferred_element_type=f32)

    def square_sums(part):
        total = jnp.zeros((TPF, LANES), f32)
        for low, width in OUT_CHUNKS:
            span = slice(part * D + low, part * D + low + width)
            values = raw[:, span]
            total = total + jnp.dot(
                (values * values).astype(bf16), picker[span, :], preferred_element_type=f32
            )
        return total

    ready(0)
    raw[:, 0:first] = product(0, 0, first)
    ready(1)
    if first < D:
        raw[:, first:D] = product(0, first, D)
    ready(2)
    raw[:, D : 2 * D] = product(1)
    squares = square_sums(0)
    ready(3)
    packed[:, 2 * D : 3 * D] = product(2).astype(bf16)
    squares = squares + square_sums(1)
    lane = iota((TPF, LANES), 1)
    head = jnp.where(lane < 2 * HEADS, lane, lane - 2 * HEADS)
    factor = lax.rsqrt(squares * (1.0 / HEAD) + norm_eps)
    factor = factor * jnp.where(head < HEADS, HEAD ** (-0.5) * math.log2(math.e), 1.0)
    coarse = factor.astype(bf16)
    fine = (factor - coarse.astype(f32)).astype(bf16)
    both = jnp.where(lane < 2 * HEADS, coarse.astype(f32), fine.astype(f32)).astype(bf16)
    for low in range(0, 2 * D, 256):
        spread = lax.dot_general(
            both,
            picker[low : low + 256, :],
            (((1,), (1,)), ((), ())),
            preferred_element_type=f32,
        )
        packed[:, low : low + 256] = (raw[:, low : low + 256] * spread).astype(bf16)


def attend(packed, attended, same):
    ones = jnp.ones((TPF, LANES), bf16)
    lane = iota((TPF, LANES), 1)
    pending = None
    for head in range(HEADS):
        start = head * HEAD
        low = start // LANES * LANES
        high = -(-(start + HEAD) // LANES) * LANES
        wide = iota((TPF, high - low), 1) + low
        inside = (wide >= start) & (wide < start + HEAD)
        queries = packed[:, low:high]
        scores = lax.dot_general(
            jnp.where(inside, queries, jnp.zeros_like(queries)),
            packed[:, D + low : D + high],
            (((1,), (1,)), ((), ())),
            preferred_element_type=f32,
        )
        weights = jnp.exp2(scores).astype(bf16)
        if same is not None:
            weights = weights * same[...]
        values = packed[:, 2 * D + low : 2 * D + high]
        single = high - low == LANES
        if single:
            values = jnp.concatenate([values, ones], 1)
        else:
            values = jnp.where(inside, values, jnp.ones_like(values))
        mixed = jnp.dot(weights, values, preferred_element_type=f32)
        left, right = mixed[:, :LANES], mixed[:, LANES:]
        before = lane < start - low
        share = 1.0 / (right if single else jnp.where(before, left, right))
        left = left * share
        if start > low:
            left = jnp.where(before, pending, left)
        pending = left if single else right * share
        if start + HEAD >= low + LANES:
            attended[:, low : low + LANES] = left.astype(bf16)


def spatial_kernel(
    step_ref, hidden_hbm, time_hbm, qkv_hbm, out_hbm,
    after_hbm,
    after_ref, hidden, modulation, gate_weight, query, key, value, out_weight, picker, normed, raw,
    packed, attended, sems,
):
    parts = (query, key, value)
    pairs = [(hidden_hbm, hidden), (time_hbm.at[:, 0 : 2 * D], modulation)]
    for low, high in ((0, FIRST), (FIRST, D)):
        pairs.append((qkv_hbm.at[:, low:high], query.at[:, low:high]))
    pairs += [(qkv_hbm.at[:, part * D : (part + 1) * D], parts[part]) for part in (1, 2)]
    pairs += [(time_hbm.at[:, 2 * D : 3 * D], gate_weight), (out_hbm, out_weight)]
    copies = copies_of(pairs, sems)

    fill_picker(picker)
    activated = embed(step_ref)
    copies[0].wait()

    def normalise(rows):
        raw[rows, 0:D] = centre(hidden[rows, :].astype(f32))

    by_rows(normalise)
    copies[1].wait()
    table = jnp.dot(activated, modulation[...], preferred_element_type=f32)
    shift, scale = table[0:1, 0:D], 1.0 + table[0:1, D : 2 * D]

    def modulate(rows):
        normed[rows, :] = (raw[rows, 0:D] * scale + shift).astype(bf16)

    by_rows(modulate)
    project(normed, parts, picker, raw, packed, lambda piece: copies[2 + piece].wait(), FIRST)
    attend(packed, attended, None)
    copies[6].wait()
    copies[7].wait()
    gate = jnp.dot(activated, gate_weight[...], preferred_element_type=f32)[0:1, :]
    sent = []
    for low, width in OUT_CHUNKS:
        projected = jnp.dot(
            attended[...], out_weight[:, low : low + width], preferred_element_type=f32
        )
        after = hidden[:, low : low + width].astype(f32) + gate[:, low : low + width] * projected
        span = slice(low, low + width)
        after_ref[:, :, span] = after.astype(bf16).reshape(TPF // 2, 2, width)
        sent.append(
            pltpu.make_async_copy(
                after_ref.at[:, :, span], after_hbm.at[:, :, span], sems.at[8 + len(sent)]
            )
        )
        sent[-1].start()
    for copy in sent:
        copy.wait()


def prepare_kernel(
    step_ref, tag_ref, level_ref, time_hbm, qkv_hbm,
    table_hbm, query_hbm, terms_hbm,
    modulation, table, terms, sems,
):
    copies = copies_of(
        [
            (time_hbm.at[:, 3 * D : 6 * D], modulation),
            (qkv_hbm.at[:, 0:D], query_hbm),
        ],
        sems,
    )
    activated = embed(step_ref)
    level = jnp.full((8, LANES), level_ref[tag_ref[0]], f32)
    time_value = jnp.full((8, LANES), step_ref[0], jnp.int32).astype(f32) / STEPS
    noise_scale = level * jnp.sqrt(time_value / (1.0 - time_value))
    spread = noise_scale * math.sqrt(1.0 / STEPS)
    terms[0:8, :] = noise_scale * noise_scale / (2.0 * time_value)
    terms[8:16, :] = 1.0 - time_value
    terms[16:24, :] = spread
    terms[24:32, :] = -jnp.log(spread)
    copies[0].wait()
    table[...] = jnp.dot(activated, modulation[...], preferred_element_type=f32)[0:8]
    results = [
        pltpu.make_async_copy(table, table_hbm, sems.at[2]),
        pltpu.make_async_copy(terms, terms_hbm, sems.at[3]),
    ]
    for copy in results:
        copy.start()
    for copy in results:
        copy.wait()
    copies[1].wait()


def temporal_kernel(
    arrived_ref, table, query, qkv_hbm, out_hbm, final_hbm,
    velocity_ref,
    picker, same, key, value, out_weight, final_weight,
    normed, raw, packed, attended, term, after, sems,
):
    copies = copies_of(
        [
            (qkv_hbm.at[:, D : 2 * D], key),
            (qkv_hbm.at[:, 2 * D : 3 * D], value),
            (out_hbm, out_weight),
            (final_hbm, final_weight),
        ],
        sems,
    )
    after[...] = arrived_ref[...].reshape(TPF, D)
    fill_picker(picker)
    parity = (iota((TPF, TPF), 0) ^ iota((TPF, TPF), 1)) & 1
    same[...] = jnp.where(parity == 0, 1.0, 0.0).astype(bf16)
    shift, scale = table[0:1, 0:D], 1.0 + table[0:1, D : 2 * D]
    gate = table[0:1, 2 * D : 3 * D]

    def modulate(rows):
        normed[rows, :] = (centre(after[rows, :].astype(f32)) * scale + shift).astype(bf16)

    by_rows(modulate)

    def ready(piece):
        if piece >= 2:
            copies[piece - 2].wait()

    project(normed, (query, key, value), picker, raw, packed, ready, D)
    attend(packed, attended, same)
    copies[2].wait()
    copies[3].wait()
    for low, width in OUT_CHUNKS:
        term[:, low : low + width] = jnp.dot(
            attended[...], out_weight[:, low : low + width], preferred_element_type=f32
        ).astype(bf16)

    def finish(rows):
        state = after[rows, :].astype(f32) + gate * term[rows, :].astype(f32)
        normed[rows, :] = centre(state).astype(bf16)

    by_rows(finish)
    velocity_ref[:, 0:C] = lax.dot_general(
        normed[...], final_weight[...], (((1,), (1,)), ((), ())), preferred_element_type=f32
    )
    velocity_ref[:, C:] = jnp.zeros((TPF, LANES - C), f32)


def density_kernel(terms_ref, velocity_ref, now_ref, next_ref, log_ref, mean_ref):
    velocity = velocity_ref[...].T[0:C, :]
    factor, rest, spread, minus_log = (terms_ref[8 * row : 8 * row + 1, 0:1] for row in range(4))
    now = now_ref[0]
    drift = velocity + factor * (now + rest * velocity)
    next_mean = now - drift / STEPS
    standard = (next_ref[0] - next_mean) / spread
    log_ref[...] = (
        -0.5 * jnp.mean(standard * standard, 0, keepdims=True)
        + minus_log
        - 0.5 * math.log(2.0 * math.pi)
    )
    mean_ref[0] = next_mean


SMEM = pl.BlockSpec(memory_space=pltpu.SMEM)
HBM = pl.BlockSpec(memory_space=pltpu.HBM)
VMEM = pl.BlockSpec(memory_space=pltpu.VMEM)
work = [
    pltpu.VMEM((TPF, D), bf16),
    pltpu.VMEM((TPF, 2 * D), f32),
    pltpu.VMEM((TPF, 3 * D), bf16),
    pltpu.VMEM((TPF, D), bf16),
]


def in_hbm(array):
    return pltpu.with_memory_space_constraint(array, pltpu.HBM)


def shards(
    hidden,
    latents_now,
    latents_next,
    timestep,
    version_tags,
    noise_levels,
    time_weight,
    spatial_qkv,
    spatial_out,
    temporal_qkv,
    temporal_out,
    final_weight,
):
    time_weight, temporal_qkv = in_hbm(time_weight), in_hbm(temporal_qkv)
    part = pltpu.VMEM((D, D), bf16)
    picker = pltpu.VMEM((2 * D, LANES), bf16)
    after_spatial = pl.pallas_call(
        spatial_kernel,
        out_shape=jax.ShapeDtypeStruct((TPF // 2, 2, D), bf16),
        in_specs=[SMEM] + [HBM] * 4,
        out_specs=HBM,
        scratch_shapes=[
            pltpu.VMEM((TPF // 2, 2, D), bf16),
            pltpu.VMEM((TPF, D), bf16),
            pltpu.VMEM((FREQ, 2 * D), bf16),
            pltpu.VMEM((FREQ, D), bf16),
            part,
            part,
            part,
            part,
            picker,
            *work,
            pltpu.SemaphoreType.DMA((8 + len(OUT_CHUNKS),)),
        ],
        compiler_params=pltpu.CompilerParams(vmem_limit_bytes=40 << 20),
        cost_estimate=pl.CostEstimate(
            flops=4 << 30, bytes_accessed=14 << 20, transcendentals=1 << 20
        ),
        name="spatial",
    )(timestep, in_hbm(hidden), time_weight, in_hbm(spatial_qkv), in_hbm(spatial_out))
    arrived = lax.all_to_all(
        after_spatial, ("inner", "outer"), split_axis=0, concat_axis=0, tiled=True
    )
    table, query, terms = pl.pallas_call(
        prepare_kernel,
        out_shape=(
            jax.ShapeDtypeStruct((8, 3 * D), f32),
            jax.ShapeDtypeStruct((D, D), bf16),
            jax.ShapeDtypeStruct((32, LANES), f32),
        ),
        in_specs=[SMEM] * 3 + [HBM] * 2,
        out_specs=(HBM, HBM, HBM),
        scratch_shapes=[
            pltpu.VMEM((FREQ, 3 * D), bf16),
            pltpu.VMEM((8, 3 * D), f32),
            pltpu.VMEM((32, LANES), f32),
            pltpu.SemaphoreType.DMA((4,)),
        ],
        compiler_params=pltpu.CompilerParams(vmem_limit_bytes=8 << 20),
        cost_estimate=pl.CostEstimate(
            flops=32 << 20, bytes_accessed=8 << 20, transcendentals=1 << 13
        ),
        name="prepare",
    )(timestep, version_tags, noise_levels, time_weight, temporal_qkv)
    velocity = pl.pallas_call(
        temporal_kernel,
        out_shape=jax.ShapeDtypeStruct((TPF, LANES), f32),
        in_specs=[VMEM] * 3 + [HBM] * 3,
        out_specs=VMEM,
        scratch_shapes=[
            picker,
            pltpu.VMEM((TPF, TPF), bf16),
            part,
            part,
            part,
            pltpu.VMEM((C, D), bf16),
            *work,
            pltpu.VMEM((TPF, D), bf16),
            pltpu.VMEM((TPF, D), bf16),
            pltpu.SemaphoreType.DMA((4,)),
        ],
        compiler_params=pltpu.CompilerParams(vmem_limit_bytes=40 << 20),
        cost_estimate=pl.CostEstimate(
            flops=4 << 30, bytes_accessed=12 << 20, transcendentals=1 << 20
        ),
        name="temporal",
    )(arrived, table, query, temporal_qkv, in_hbm(temporal_out), in_hbm(final_weight))
    returned = lax.all_to_all(
        velocity.reshape(TPF // 2, 2, LANES),
        ("inner", "outer"),
        split_axis=0,
        concat_axis=0,
        tiled=True,
    )
    return pl.pallas_call(
        density_kernel,
        out_shape=(
            jax.ShapeDtypeStruct((1, TPF), f32),
            jax.ShapeDtypeStruct((1, C, TPF), f32),
        ),
        in_specs=[VMEM] * 4,
        out_specs=(VMEM, VMEM),
        compiler_params=pltpu.CompilerParams(vmem_limit_bytes=4 << 20),
        name="density",
    )(terms, returned.reshape(TPF, LANES), latents_now, latents_next)


def solution(mesh):
    return jax.shard_map(
        shards,
        mesh=mesh,
        in_specs=(
            P(("inner", "outer"), None),
            P(("inner", "outer"), None, None),
            P(("inner", "outer"), None, None),
            P(),
            P(("inner", "outer")),
            P(),
            P(),
            P(),
            P(),
            P(),
            P(),
            P(),
        ),
        out_specs=(P(("inner", "outer"), None), P(("inner", "outer"), None, None)),
        check_vma=False,
    )
```

```python
import math

import jax
import jax.numpy as jnp
from jax import lax
from jax.experimental import pallas as pl
from jax.experimental.pallas import tpu as pltpu
from jax.sharding import PartitionSpec as P

D = 1152
HEADS = 16
HEAD = D // HEADS
C = 16
FREQ = 256
STEPS = 10
VERSIONS = 8
TPF = 256
LANES = 128
OUT_CHUNKS = tuple((low, min(512, D - low)) for low in range(0, D, 512))
CUTS = (0, 512, 1280, 2 * D, 3 * D)
EARLY = 1024
ROWS = 32

norm_eps = 1e-06
f32 = jnp.float32
bf16 = jnp.bfloat16


def iota(shape, dim):
    return lax.broadcasted_iota(jnp.int32, shape, dim)


def centre(values):
    centred = values - jnp.mean(values, -1, keepdims=True)
    variance = jnp.mean(centred * centred, -1, keepdims=True)
    return centred * lax.rsqrt(variance + norm_eps)


def fill_picker(picker):
    for low in range(0, 2 * D, 256):
        offset = iota((256, LANES), 0) + low - iota((256, LANES), 1) * HEAD
        inside = (offset >= 0) & (offset < HEAD)
        picker[low : low + 256, :] = jnp.where(inside, 1.0, 0.0).astype(bf16)


def by_rows(step):
    def one(index, carry):
        step(pl.ds(pl.multiple_of(index * ROWS, ROWS), ROWS))
        return carry

    lax.fori_loop(0, TPF // ROWS, one, 0, unroll=True)


def embed(step_ref):
    time_value = jnp.full((16, FREQ // 2), step_ref[0], jnp.int32).astype(f32) / STEPS
    position = iota((16, FREQ // 2), 1).astype(f32)
    angles = 1000.0 * time_value * jnp.exp(-math.log(10000.0) * position / (FREQ // 2))
    embedded = jnp.concatenate([jnp.cos(angles), jnp.sin(angles)], 1)
    return (embedded / (1.0 + jnp.exp(-embedded))).astype(bf16)


def copies_of(pairs, sems):
    copies = [
        pltpu.make_async_copy(source, target, sems.at[index])
        for index, (source, target) in enumerate(pairs)
    ]
    for copy in copies:
        copy.start()
    return copies


def project(normed, pieces, picker, packed):
    squares = jnp.zeros((TPF, LANES), f32)
    before = None
    for low, high, weight, wait in pieces:
        wait()
        mixed = jnp.dot(normed[...], weight[...], preferred_element_type=f32)
        packed[:, low:high] = mixed.astype(bf16)
        if before:
            for left in range(before[0], before[1], 512):
                span = slice(left, min(left + 512, before[1]))
                values = packed[:, span].astype(f32)
                squares = squares + jnp.dot(
                    (values * values).astype(bf16), picker[span, :], preferred_element_type=f32
                )
        before = (low, high)
    factor = lax.rsqrt(squares * (1.0 / HEAD) + norm_eps)
    lane = iota((TPF, LANES), 1)
    return factor * jnp.where(lane < HEADS, HEAD ** (-0.5) * math.log2(math.e), 1.0)


def attend(packed, factor, attended, same):
    across = factor.T
    ones = jnp.ones((TPF, LANES), bf16)
    lane = iota((TPF, LANES), 1)
    pending = None
    for head in range(HEADS):
        start = head * HEAD
        low = start // LANES * LANES
        high = -(-(start + HEAD) // LANES) * LANES
        wide = iota((TPF, high - low), 1) + low
        inside = (wide >= start) & (wide < start + HEAD)
        queries = packed[:, low:high]
        scores = lax.dot_general(
            jnp.where(inside, queries, jnp.zeros_like(queries)),
            packed[:, D + low : D + high],
            (((1,), (1,)), ((), ())),
            preferred_element_type=f32,
        )
        scores = scores * factor[:, head : head + 1]
        scores = scores * across[HEADS + head : HEADS + head + 1, :]
        weights = jnp.exp2(scores).astype(bf16)
        if same is not None:
            weights = weights * same[...]
        values = packed[:, 2 * D + low : 2 * D + high]
        single = high - low == LANES
        if single:
            values = jnp.concatenate([values, ones], 1)
        else:
            values = jnp.where(inside, values, jnp.ones_like(values))
        mixed = jnp.dot(weights, values, preferred_element_type=f32)
        left, right = mixed[:, :LANES], mixed[:, LANES:]
        before = lane < start - low
        share = 1.0 / (right if single else jnp.where(before, left, right))
        left = left * share
        if start > low:
            left = jnp.where(before, pending, left)
        pending = left if single else right * share
        if start + HEAD >= low + LANES:
            attended[:, low : low + LANES] = left.astype(bf16)


def spatial_kernel(
    step_ref, hidden_hbm, time_hbm, qkv_hbm, out_hbm,
    after_hbm,
    after_ref, hidden, modulation, gate_weight, out_weight, picker, raw, normed, packed, attended,
    sems, *parts,
):
    pairs = [(hidden_hbm, hidden), (time_hbm.at[:, 0 : 2 * D], modulation)]
    pairs += [
        (qkv_hbm.at[:, low:high], part) for low, high, part in zip(CUTS, CUTS[1:], parts)
    ]
    pairs += [(time_hbm.at[:, 2 * D : 3 * D], gate_weight), (out_hbm, out_weight)]
    copies = copies_of(pairs, sems)

    fill_picker(picker)
    activated = embed(step_ref)
    copies[0].wait()

    def normalise(rows):
        raw[rows, 0:D] = centre(hidden[rows, :].astype(f32))

    by_rows(normalise)
    copies[1].wait()
    table = jnp.dot(activated, modulation[...], preferred_element_type=f32)
    shift, scale = table[0:1, 0:D], 1.0 + table[0:1, D : 2 * D]

    def modulate(rows):
        normed[rows, :] = (raw[rows, 0:D] * scale + shift).astype(bf16)

    by_rows(modulate)
    waits = [copy.wait for copy in copies[2:6]]
    factor = project(normed, list(zip(CUTS, CUTS[1:], parts, waits)), picker, packed)
    attend(packed, factor, attended, None)
    copies[6].wait()
    copies[7].wait()
    gate = jnp.dot(activated, gate_weight[...], preferred_element_type=f32)[0:1, :]
    sent = []
    for low, width in OUT_CHUNKS:
        projected = jnp.dot(
            attended[...], out_weight[:, low : low + width], preferred_element_type=f32
        )
        after = hidden[:, low : low + width].astype(f32) + gate[:, low : low + width] * projected
        span = slice(low, low + width)
        after_ref[:, :, span] = after.astype(bf16).reshape(TPF // 2, 2, width)
        sent.append(
            pltpu.make_async_copy(
                after_ref.at[:, :, span], after_hbm.at[:, :, span], sems.at[8 + len(sent)]
            )
        )
        sent[-1].start()
    for copy in sent:
        copy.wait()


def prepare_kernel(
    step_ref, tag_ref, level_ref, time_hbm, qkv_hbm,
    table_hbm, early_hbm, terms_hbm,
    modulation, table, terms, sems,
):
    copies = copies_of(
        [
            (time_hbm.at[:, 3 * D : 6 * D], modulation),
            (qkv_hbm.at[:, 0:EARLY], early_hbm),
        ],
        sems,
    )
    activated = embed(step_ref)
    level = jnp.full((8, LANES), level_ref[tag_ref[0]], f32)
    time_value = jnp.full((8, LANES), step_ref[0], jnp.int32).astype(f32) / STEPS
    noise_scale = level * jnp.sqrt(time_value / (1.0 - time_value))
    spread = noise_scale * math.sqrt(1.0 / STEPS)
    terms[0:8, :] = noise_scale * noise_scale / (2.0 * time_value)
    terms[8:16, :] = 1.0 - time_value
    terms[16:24, :] = spread
    terms[24:32, :] = -jnp.log(spread)
    copies[0].wait()
    table[...] = jnp.dot(activated, modulation[...], preferred_element_type=f32)[0:8]
    results = [
        pltpu.make_async_copy(table, table_hbm, sems.at[2]),
        pltpu.make_async_copy(terms, terms_hbm, sems.at[3]),
    ]
    for copy in results:
        copy.start()
    for copy in results:
        copy.wait()
    copies[1].wait()


def temporal_kernel(
    arrived_ref, table, early, qkv_hbm, out_hbm, final_hbm,
    velocity_ref,
    picker, same, middle, value, out_weight, final_weight,
    normed, packed, attended, term, after, sems,
):
    copies = copies_of(
        [
            (qkv_hbm.at[:, EARLY : 2 * D], middle),
            (qkv_hbm.at[:, 2 * D : 3 * D], value),
            (out_hbm, out_weight),
            (final_hbm, final_weight),
        ],
        sems,
    )
    after[...] = arrived_ref[...].reshape(TPF, D)
    fill_picker(picker)
    parity = (iota((TPF, TPF), 0) ^ iota((TPF, TPF), 1)) & 1
    same[...] = jnp.where(parity == 0, 1.0, 0.0).astype(bf16)
    shift, scale = table[0:1, 0:D], 1.0 + table[0:1, D : 2 * D]
    gate = table[0:1, 2 * D : 3 * D]

    def modulate(rows):
        normed[rows, :] = (centre(after[rows, :].astype(f32)) * scale + shift).astype(bf16)

    by_rows(modulate)

    pieces = [
        (0, EARLY, early, lambda: None),
        (EARLY, 2 * D, middle, copies[0].wait),
        (2 * D, 3 * D, value, copies[1].wait),
    ]
    factor = project(normed, pieces, picker, packed)
    attend(packed, factor, attended, same)
    copies[2].wait()
    copies[3].wait()
    for low, width in OUT_CHUNKS:
        term[:, low : low + width] = jnp.dot(
            attended[...], out_weight[:, low : low + width], preferred_element_type=f32
        ).astype(bf16)

    def finish(rows):
        state = after[rows, :].astype(f32) + gate * term[rows, :].astype(f32)
        normed[rows, :] = centre(state).astype(bf16)

    by_rows(finish)
    velocity_ref[:, 0:C] = lax.dot_general(
        normed[...], final_weight[...], (((1,), (1,)), ((), ())), preferred_element_type=f32
    )
    velocity_ref[:, C:] = jnp.zeros((TPF, LANES - C), f32)


def density_kernel(terms_ref, velocity_ref, now_ref, next_ref, log_ref, mean_ref):
    velocity = velocity_ref[...].T[0:C, :]
    factor, rest, spread, minus_log = (terms_ref[8 * row : 8 * row + 1, 0:1] for row in range(4))
    now = now_ref[0]
    drift = velocity + factor * (now + rest * velocity)
    next_mean = now - drift / STEPS
    standard = (next_ref[0] - next_mean) / spread
    log_ref[...] = (
        -0.5 * jnp.mean(standard * standard, 0, keepdims=True)
        + minus_log
        - 0.5 * math.log(2.0 * math.pi)
    )
    mean_ref[0] = next_mean


SMEM = pl.BlockSpec(memory_space=pltpu.SMEM)
HBM = pl.BlockSpec(memory_space=pltpu.HBM)
VMEM = pl.BlockSpec(memory_space=pltpu.VMEM)
work = [
    pltpu.VMEM((TPF, D), bf16),
    pltpu.VMEM((TPF, 3 * D), bf16),
    pltpu.VMEM((TPF, D), bf16),
]


def in_hbm(array):
    return pltpu.with_memory_space_constraint(array, pltpu.HBM)


def shards(
    hidden,
    latents_now,
    latents_next,
    timestep,
    version_tags,
    noise_levels,
    time_weight,
    spatial_qkv,
    spatial_out,
    temporal_qkv,
    temporal_out,
    final_weight,
):
    time_weight, temporal_qkv = in_hbm(time_weight), in_hbm(temporal_qkv)
    picker = pltpu.VMEM((2 * D, LANES), bf16)
    after_spatial = pl.pallas_call(
        spatial_kernel,
        out_shape=jax.ShapeDtypeStruct((TPF // 2, 2, D), bf16),
        in_specs=[SMEM] + [HBM] * 4,
        out_specs=HBM,
        scratch_shapes=[
            pltpu.VMEM((TPF // 2, 2, D), bf16),
            pltpu.VMEM((TPF, D), bf16),
            pltpu.VMEM((FREQ, 2 * D), bf16),
            pltpu.VMEM((FREQ, D), bf16),
            pltpu.VMEM((D, D), bf16),
            picker,
            pltpu.VMEM((TPF, D), f32),
            *work,
            pltpu.SemaphoreType.DMA((8 + len(OUT_CHUNKS),)),
            *(pltpu.VMEM((D, high - low), bf16) for low, high in zip(CUTS, CUTS[1:])),
        ],
        compiler_params=pltpu.CompilerParams(vmem_limit_bytes=40 << 20),
        cost_estimate=pl.CostEstimate(
            flops=4 << 30, bytes_accessed=14 << 20, transcendentals=1 << 20
        ),
        name="spatial",
    )(timestep, in_hbm(hidden), time_weight, in_hbm(spatial_qkv), in_hbm(spatial_out))
    arrived = lax.all_to_all(
        after_spatial, ("inner", "outer"), split_axis=0, concat_axis=0, tiled=True
    )
    table, early, terms = pl.pallas_call(
        prepare_kernel,
        out_shape=(
            jax.ShapeDtypeStruct((8, 3 * D), f32),
            jax.ShapeDtypeStruct((D, EARLY), bf16),
            jax.ShapeDtypeStruct((32, LANES), f32),
        ),
        in_specs=[SMEM] * 3 + [HBM] * 2,
        out_specs=(HBM, HBM, HBM),
        scratch_shapes=[
            pltpu.VMEM((FREQ, 3 * D), bf16),
            pltpu.VMEM((8, 3 * D), f32),
            pltpu.VMEM((32, LANES), f32),
            pltpu.SemaphoreType.DMA((4,)),
        ],
        compiler_params=pltpu.CompilerParams(vmem_limit_bytes=8 << 20),
        cost_estimate=pl.CostEstimate(
            flops=32 << 20, bytes_accessed=8 << 20, transcendentals=1 << 13
        ),
        name="prepare",
    )(timestep, version_tags, noise_levels, time_weight, temporal_qkv)
    velocity = pl.pallas_call(
        temporal_kernel,
        out_shape=jax.ShapeDtypeStruct((TPF, LANES), f32),
        in_specs=[VMEM] * 3 + [HBM] * 3,
        out_specs=VMEM,
        scratch_shapes=[
            picker,
            pltpu.VMEM((TPF, TPF), bf16),
            pltpu.VMEM((D, 2 * D - EARLY), bf16),
            pltpu.VMEM((D, D), bf16),
            pltpu.VMEM((D, D), bf16),
            pltpu.VMEM((C, D), bf16),
            *work,
            pltpu.VMEM((TPF, D), bf16),
            pltpu.VMEM((TPF, D), bf16),
            pltpu.SemaphoreType.DMA((4,)),
        ],
        compiler_params=pltpu.CompilerParams(vmem_limit_bytes=40 << 20),
        cost_estimate=pl.CostEstimate(
            flops=4 << 30, bytes_accessed=12 << 20, transcendentals=1 << 20
        ),
        name="temporal",
    )(arrived, table, early, temporal_qkv, in_hbm(temporal_out), in_hbm(final_weight))
    returned = lax.all_to_all(
        velocity.reshape(TPF // 2, 2, LANES),
        ("inner", "outer"),
        split_axis=0,
        concat_axis=0,
        tiled=True,
    )
    return pl.pallas_call(
        density_kernel,
        out_shape=(
            jax.ShapeDtypeStruct((1, TPF), f32),
            jax.ShapeDtypeStruct((1, C, TPF), f32),
        ),
        in_specs=[VMEM] * 4,
        out_specs=(VMEM, VMEM),
        compiler_params=pltpu.CompilerParams(vmem_limit_bytes=4 << 20),
        name="density",
    )(terms, returned.reshape(TPF, LANES), latents_now, latents_next)


def solution(mesh):
    return jax.shard_map(
        shards,
        mesh=mesh,
        in_specs=(
            P(("inner", "outer"), None),
            P(("inner", "outer"), None, None),
            P(("inner", "outer"), None, None),
            P(),
            P(("inner", "outer")),
            P(),
            P(),
            P(),
            P(),
            P(),
            P(),
            P(),
        ),
        out_specs=(P(("inner", "outer"), None), P(("inner", "outer"), None, None)),
        check_vma=False,
    )
```

```python
import math

import jax
import jax.numpy as jnp
from jax import lax
from jax.experimental import pallas as pl
from jax.experimental.pallas import tpu as pltpu
from jax.sharding import PartitionSpec as P

D = 1152
HEADS = 16
HEAD = D // HEADS
C = 16
FREQ = 256
STEPS = 10
VERSIONS = 8
TPF = 256
LANES = 128
OUT_CHUNKS = tuple((low, min(512, D - low)) for low in range(0, D, 512))
CUTS = (0, 512, 1280, 2 * D, 3 * D)
EARLY = 1024
ROWS = 32

norm_eps = 1e-06
f32 = jnp.float32
bf16 = jnp.bfloat16


def iota(shape, dim):
    return lax.broadcasted_iota(jnp.int32, shape, dim)


def centre(values):
    centred = values - jnp.mean(values, -1, keepdims=True)
    variance = jnp.mean(centred * centred, -1, keepdims=True)
    return centred * lax.rsqrt(variance + norm_eps)


def fill_picker(picker):
    for low in range(0, 2 * D, 256):
        offset = iota((256, LANES), 0) + low - iota((256, LANES), 1) * HEAD
        inside = (offset >= 0) & (offset < HEAD)
        picker[low : low + 256, :] = jnp.where(inside, 1.0, 0.0).astype(bf16)


def by_rows(step):
    def one(index, carry):
        step(pl.ds(pl.multiple_of(index * ROWS, ROWS), ROWS))
        return carry

    lax.fori_loop(0, TPF // ROWS, one, 0, unroll=True)


def embed(step_ref):
    time_value = jnp.full((16, FREQ // 2), step_ref[0], jnp.int32).astype(f32) / STEPS
    position = iota((16, FREQ // 2), 1).astype(f32)
    angles = 1000.0 * time_value * jnp.exp(-math.log(10000.0) * position / (FREQ // 2))
    embedded = jnp.concatenate([jnp.cos(angles), jnp.sin(angles)], 1)
    return (embedded / (1.0 + jnp.exp(-embedded))).astype(bf16)


def copies_of(pairs, sems):
    copies = [
        pltpu.make_async_copy(source, target, sems.at[index])
        for index, (source, target) in enumerate(pairs)
    ]
    for copy in copies:
        copy.start()
    return copies


def project(normed, pieces, picker, packed):
    squares = jnp.zeros((TPF, LANES), f32)
    before = None
    for low, high, weight, wait in pieces:
        wait()
        mixed = jnp.dot(normed[...], weight[...], preferred_element_type=f32)
        packed[:, low:high] = mixed.astype(bf16)
        if before:
            for left in range(before[0], before[1], 512):
                span = slice(left, min(left + 512, before[1]))
                values = packed[:, span].astype(f32)
                squares = squares + jnp.dot(
                    (values * values).astype(bf16), picker[span, :], preferred_element_type=f32
                )
        before = (low, high)
    factor = lax.rsqrt(squares * (1.0 / HEAD) + norm_eps)
    lane = iota((TPF, LANES), 1)
    return factor * jnp.where(lane < HEADS, HEAD ** (-0.5) * math.log2(math.e), 1.0)


def attend(packed, factor, attended, same):
    across = factor.T
    ones = jnp.ones((TPF, LANES), bf16)
    lane = iota((TPF, LANES), 1)
    pending = None
    for head in range(HEADS):
        start = head * HEAD
        low = start // LANES * LANES
        high = -(-(start + HEAD) // LANES) * LANES
        wide = iota((TPF, high - low), 1) + low
        inside = (wide >= start) & (wide < start + HEAD)
        queries = packed[:, low:high]
        scores = lax.dot_general(
            jnp.where(inside, queries, jnp.zeros_like(queries)),
            packed[:, D + low : D + high],
            (((1,), (1,)), ((), ())),
            preferred_element_type=f32,
        )
        scores = scores * factor[:, head : head + 1]
        scores = scores * across[HEADS + head : HEADS + head + 1, :]
        weights = jnp.exp2(scores).astype(bf16)
        if same is not None:
            weights = weights * same[...]
        values = packed[:, 2 * D + low : 2 * D + high]
        single = high - low == LANES
        if single:
            values = jnp.concatenate([values, ones], 1)
        else:
            values = jnp.where(inside, values, jnp.ones_like(values))
        mixed = jnp.dot(weights, values, preferred_element_type=f32)
        left, right = mixed[:, :LANES], mixed[:, LANES:]
        before = lane < start - low
        share = 1.0 / (right if single else jnp.where(before, left, right))
        left = left * share
        if start > low:
            left = jnp.where(before, pending, left)
        pending = left if single else right * share
        if start + HEAD >= low + LANES:
            attended[:, low : low + LANES] = left.astype(bf16)


def spatial_kernel(
    step_ref, hidden_hbm, time_hbm, qkv_hbm, out_hbm,
    after_hbm,
    after_ref, hidden, modulation, gate_weight, out_weight, picker, raw, normed, packed, attended,
    sems, *parts,
):
    pairs = [(hidden_hbm, hidden), (time_hbm.at[:, 0 : 2 * D], modulation)]
    pairs += [
        (qkv_hbm.at[:, low:high], part) for low, high, part in zip(CUTS, CUTS[1:], parts)
    ]
    pairs += [(time_hbm.at[:, 2 * D : 3 * D], gate_weight), (out_hbm, out_weight)]
    copies = copies_of(pairs, sems)

    fill_picker(picker)
    activated = embed(step_ref)
    copies[0].wait()

    def normalise(rows):
        raw[rows, 0:D] = centre(hidden[rows, :].astype(f32))

    by_rows(normalise)
    copies[1].wait()
    table = jnp.dot(activated, modulation[...], preferred_element_type=f32)
    shift, scale = table[0:1, 0:D], 1.0 + table[0:1, D : 2 * D]

    def modulate(rows):
        normed[rows, :] = (raw[rows, 0:D] * scale + shift).astype(bf16)

    by_rows(modulate)
    waits = [copy.wait for copy in copies[2:6]]
    factor = project(normed, list(zip(CUTS, CUTS[1:], parts, waits)), picker, packed)
    attend(packed, factor, attended, None)
    copies[6].wait()
    copies[7].wait()
    gate = jnp.dot(activated, gate_weight[...], preferred_element_type=f32)[0:1, :]
    sent = []
    for low, width in OUT_CHUNKS:
        projected = jnp.dot(
            attended[...], out_weight[:, low : low + width], preferred_element_type=f32
        )
        after = hidden[:, low : low + width].astype(f32) + gate[:, low : low + width] * projected
        span = slice(low, low + width)
        after_ref[:, :, span] = after.astype(bf16).reshape(TPF // 2, 2, width)
        sent.append(
            pltpu.make_async_copy(
                after_ref.at[:, :, span], after_hbm.at[:, :, span], sems.at[8 + len(sent)]
            )
        )
        sent[-1].start()
    for copy in sent:
        copy.wait()


def prepare_kernel(
    step_ref, tag_ref, level_ref, time_hbm, qkv_hbm, final_hbm,
    table_hbm, early_hbm, terms_hbm, head_hbm,
    modulation, final_weight, table, terms, head_weight, sems,
):
    copies = copies_of(
        [
            (time_hbm.at[:, 3 * D : 6 * D], modulation),
            (qkv_hbm.at[:, 0:EARLY], early_hbm),
            (final_hbm, final_weight),
        ],
        sems,
    )
    activated = embed(step_ref)
    level = jnp.full((8, LANES), level_ref[tag_ref[0]], f32)
    time_value = jnp.full((8, LANES), step_ref[0], jnp.int32).astype(f32) / STEPS
    noise_scale = level * jnp.sqrt(time_value / (1.0 - time_value))
    spread = noise_scale * math.sqrt(1.0 / STEPS)
    terms[0:8, :] = noise_scale * noise_scale / (2.0 * time_value)
    terms[8:16, :] = 1.0 - time_value
    terms[16:24, :] = spread
    terms[24:32, :] = -jnp.log(spread)
    copies[0].wait()
    table[...] = jnp.dot(activated, modulation[...], preferred_element_type=f32)[0:8]
    copies[2].wait()
    padded = jnp.concatenate([final_weight[...].astype(f32), jnp.zeros((LANES - C, D), f32)], 0)
    head_weight[...] = padded.T.astype(bf16)
    results = [
        pltpu.make_async_copy(table, table_hbm, sems.at[3]),
        pltpu.make_async_copy(terms, terms_hbm, sems.at[4]),
        pltpu.make_async_copy(head_weight, head_hbm, sems.at[5]),
    ]
    for copy in results:
        copy.start()
    for copy in results:
        copy.wait()
    copies[1].wait()


def temporal_kernel(
    arrived_ref, table, early, head_weight, qkv_hbm, out_hbm,
    velocity_ref,
    picker, same, middle, value, out_weight,
    normed, packed, attended, term, after, sems,
):
    copies = copies_of(
        [
            (qkv_hbm.at[:, EARLY : 2 * D], middle),
            (qkv_hbm.at[:, 2 * D : 3 * D], value),
            (out_hbm, out_weight),
        ],
        sems,
    )
    after[...] = arrived_ref[...].reshape(TPF, D)
    fill_picker(picker)
    parity = (iota((TPF, TPF), 0) ^ iota((TPF, TPF), 1)) & 1
    same[...] = jnp.where(parity == 0, 1.0, 0.0).astype(bf16)
    shift, scale = table[0:1, 0:D], 1.0 + table[0:1, D : 2 * D]
    gate = table[0:1, 2 * D : 3 * D]

    def modulate(rows):
        normed[rows, :] = (centre(after[rows, :].astype(f32)) * scale + shift).astype(bf16)

    by_rows(modulate)

    pieces = [
        (0, EARLY, early, lambda: None),
        (EARLY, 2 * D, middle, copies[0].wait),
        (2 * D, 3 * D, value, copies[1].wait),
    ]
    factor = project(normed, pieces, picker, packed)
    attend(packed, factor, attended, same)
    copies[2].wait()
    for low, width in OUT_CHUNKS:
        term[:, low : low + width] = jnp.dot(
            attended[...], out_weight[:, low : low + width], preferred_element_type=f32
        ).astype(bf16)

    def finish(rows):
        state = after[rows, :].astype(f32) + gate * term[rows, :].astype(f32)
        normed[rows, :] = centre(state).astype(bf16)

    by_rows(finish)
    velocity_ref[...] = jnp.dot(normed[...], head_weight[...], preferred_element_type=f32)


def density_kernel(terms_ref, velocity_ref, now_ref, next_ref, log_ref, mean_ref):
    velocity = velocity_ref[...].T[0:C, :]
    factor, rest, spread, minus_log = (terms_ref[8 * row : 8 * row + 1, 0:1] for row in range(4))
    now = now_ref[0]
    drift = velocity + factor * (now + rest * velocity)
    next_mean = now - drift / STEPS
    standard = (next_ref[0] - next_mean) / spread
    log_ref[...] = (
        -0.5 * jnp.mean(standard * standard, 0, keepdims=True)
        + minus_log
        - 0.5 * math.log(2.0 * math.pi)
    )
    mean_ref[0] = next_mean


SMEM = pl.BlockSpec(memory_space=pltpu.SMEM)
HBM = pl.BlockSpec(memory_space=pltpu.HBM)
VMEM = pl.BlockSpec(memory_space=pltpu.VMEM)
work = [
    pltpu.VMEM((TPF, D), bf16),
    pltpu.VMEM((TPF, 3 * D), bf16),
    pltpu.VMEM((TPF, D), bf16),
]


def in_hbm(array):
    return pltpu.with_memory_space_constraint(array, pltpu.HBM)


def shards(
    hidden,
    latents_now,
    latents_next,
    timestep,
    version_tags,
    noise_levels,
    time_weight,
    spatial_qkv,
    spatial_out,
    temporal_qkv,
    temporal_out,
    final_weight,
):
    time_weight, temporal_qkv = in_hbm(time_weight), in_hbm(temporal_qkv)
    picker = pltpu.VMEM((2 * D, LANES), bf16)
    after_spatial = pl.pallas_call(
        spatial_kernel,
        out_shape=jax.ShapeDtypeStruct((TPF // 2, 2, D), bf16),
        in_specs=[SMEM] + [HBM] * 4,
        out_specs=HBM,
        scratch_shapes=[
            pltpu.VMEM((TPF // 2, 2, D), bf16),
            pltpu.VMEM((TPF, D), bf16),
            pltpu.VMEM((FREQ, 2 * D), bf16),
            pltpu.VMEM((FREQ, D), bf16),
            pltpu.VMEM((D, D), bf16),
            picker,
            pltpu.VMEM((TPF, D), f32),
            *work,
            pltpu.SemaphoreType.DMA((8 + len(OUT_CHUNKS),)),
            *(pltpu.VMEM((D, high - low), bf16) for low, high in zip(CUTS, CUTS[1:])),
        ],
        compiler_params=pltpu.CompilerParams(vmem_limit_bytes=40 << 20),
        cost_estimate=pl.CostEstimate(
            flops=4 << 30, bytes_accessed=14 << 20, transcendentals=1 << 20
        ),
        name="spatial",
    )(timestep, in_hbm(hidden), time_weight, in_hbm(spatial_qkv), in_hbm(spatial_out))
    arrived = lax.all_to_all(
        after_spatial, ("inner", "outer"), split_axis=0, concat_axis=0, tiled=True
    )
    table, early, terms, head_weight = pl.pallas_call(
        prepare_kernel,
        out_shape=(
            jax.ShapeDtypeStruct((8, 3 * D), f32),
            jax.ShapeDtypeStruct((D, EARLY), bf16),
            jax.ShapeDtypeStruct((32, LANES), f32),
            jax.ShapeDtypeStruct((D, LANES), bf16),
        ),
        in_specs=[SMEM] * 3 + [HBM] * 3,
        out_specs=(HBM, HBM, HBM, HBM),
        scratch_shapes=[
            pltpu.VMEM((FREQ, 3 * D), bf16),
            pltpu.VMEM((C, D), bf16),
            pltpu.VMEM((8, 3 * D), f32),
            pltpu.VMEM((32, LANES), f32),
            pltpu.VMEM((D, LANES), bf16),
            pltpu.SemaphoreType.DMA((6,)),
        ],
        compiler_params=pltpu.CompilerParams(vmem_limit_bytes=8 << 20),
        cost_estimate=pl.CostEstimate(
            flops=32 << 20, bytes_accessed=8 << 20, transcendentals=1 << 13
        ),
        name="prepare",
    )(timestep, version_tags, noise_levels, time_weight, temporal_qkv, in_hbm(final_weight))
    velocity = pl.pallas_call(
        temporal_kernel,
        out_shape=jax.ShapeDtypeStruct((TPF, LANES), f32),
        in_specs=[VMEM] * 4 + [HBM] * 2,
        out_specs=VMEM,
        scratch_shapes=[
            picker,
            pltpu.VMEM((TPF, TPF), bf16),
            pltpu.VMEM((D, 2 * D - EARLY), bf16),
            pltpu.VMEM((D, D), bf16),
            pltpu.VMEM((D, D), bf16),
            *work,
            pltpu.VMEM((TPF, D), bf16),
            pltpu.VMEM((TPF, D), bf16),
            pltpu.SemaphoreType.DMA((3,)),
        ],
        compiler_params=pltpu.CompilerParams(vmem_limit_bytes=40 << 20),
        cost_estimate=pl.CostEstimate(
            flops=4 << 30, bytes_accessed=12 << 20, transcendentals=1 << 20
        ),
        name="temporal",
    )(arrived, table, early, head_weight, temporal_qkv, in_hbm(temporal_out))
    returned = lax.all_to_all(
        velocity.reshape(TPF // 2, 2, LANES),
        ("inner", "outer"),
        split_axis=0,
        concat_axis=0,
        tiled=True,
    )
    return pl.pallas_call(
        density_kernel,
        out_shape=(
            jax.ShapeDtypeStruct((1, TPF), f32),
            jax.ShapeDtypeStruct((1, C, TPF), f32),
        ),
        in_specs=[VMEM] * 4,
        out_specs=(VMEM, VMEM),
        compiler_params=pltpu.CompilerParams(vmem_limit_bytes=4 << 20),
        name="density",
    )(terms, returned.reshape(TPF, LANES), latents_now, latents_next)


def solution(mesh):
    return jax.shard_map(
        shards,
        mesh=mesh,
        in_specs=(
            P(("inner", "outer"), None),
            P(("inner", "outer"), None, None),
            P(("inner", "outer"), None, None),
            P(),
            P(("inner", "outer")),
            P(),
            P(),
            P(),
            P(),
            P(),
            P(),
            P(),
        ),
        out_specs=(P(("inner", "outer"), None), P(("inner", "outer"), None, None)),
        check_vma=False,
    )
```

```python
import math

import jax
import jax.numpy as jnp
from jax import lax
from jax.experimental import pallas as pl
from jax.experimental.pallas import tpu as pltpu
from jax.sharding import PartitionSpec as P

D = 1152
HEADS = 16
HEAD = D // HEADS
C = 16
FREQ = 256
STEPS = 10
VERSIONS = 8
TPF = 256
LANES = 128
OUT_CHUNKS = tuple((low, min(512, D - low)) for low in range(0, D, 512))
CUTS = (0, 256, 1024, 2 * D, 3 * D)
EARLY = 1024
ROWS = 32

norm_eps = 1e-06
f32 = jnp.float32
bf16 = jnp.bfloat16


def iota(shape, dim):
    return lax.broadcasted_iota(jnp.int32, shape, dim)


def centre(values):
    centred = values - jnp.mean(values, -1, keepdims=True)
    variance = jnp.mean(centred * centred, -1, keepdims=True)
    return centred * lax.rsqrt(variance + norm_eps)


def fill_picker(picker):
    for low in range(0, 2 * D, 256):
        offset = iota((256, LANES), 0) + low - iota((256, LANES), 1) * HEAD
        inside = (offset >= 0) & (offset < HEAD)
        picker[low : low + 256, :] = jnp.where(inside, 1.0, 0.0).astype(bf16)


def by_rows(step):
    def one(index, carry):
        step(pl.ds(pl.multiple_of(index * ROWS, ROWS), ROWS))
        return carry

    lax.fori_loop(0, TPF // ROWS, one, 0, unroll=True)


def embed(step_ref):
    time_value = jnp.full((16, FREQ // 2), step_ref[0], jnp.int32).astype(f32) / STEPS
    position = iota((16, FREQ // 2), 1).astype(f32)
    angles = 1000.0 * time_value * jnp.exp(-math.log(10000.0) * position / (FREQ // 2))
    embedded = jnp.concatenate([jnp.cos(angles), jnp.sin(angles)], 1)
    return (embedded / (1.0 + jnp.exp(-embedded))).astype(bf16)


def copies_of(pairs, sems):
    copies = [
        pltpu.make_async_copy(source, target, sems.at[index])
        for index, (source, target) in enumerate(pairs)
    ]
    for copy in copies:
        copy.start()
    return copies


def project(normed, pieces, picker, packed):
    squares = jnp.zeros((TPF, LANES), f32)
    before = None
    for low, high, weight, wait in pieces:
        wait()
        mixed = jnp.dot(normed[...], weight[...], preferred_element_type=f32)
        packed[:, low:high] = mixed.astype(bf16)
        if before:
            for left in range(before[0], before[1], 512):
                span = slice(left, min(left + 512, before[1]))
                values = packed[:, span].astype(f32)
                squares = squares + jnp.dot(
                    (values * values).astype(bf16), picker[span, :], preferred_element_type=f32
                )
        before = (low, high)
    factor = lax.rsqrt(squares * (1.0 / HEAD) + norm_eps)
    lane = iota((TPF, LANES), 1)
    return factor * jnp.where(lane < HEADS, HEAD ** (-0.5) * math.log2(math.e), 1.0)


def attend(packed, factor, attended, same):
    across = factor.T
    ones = jnp.ones((TPF, LANES), bf16)
    lane = iota((TPF, LANES), 1)
    pending = None
    for head in range(HEADS):
        start = head * HEAD
        low = start // LANES * LANES
        high = -(-(start + HEAD) // LANES) * LANES
        wide = iota((TPF, high - low), 1) + low
        inside = (wide >= start) & (wide < start + HEAD)
        queries = packed[:, low:high]
        scores = lax.dot_general(
            jnp.where(inside, queries, jnp.zeros_like(queries)),
            packed[:, D + low : D + high],
            (((1,), (1,)), ((), ())),
            preferred_element_type=f32,
        )
        scores = scores * factor[:, head : head + 1]
        scores = scores * across[HEADS + head : HEADS + head + 1, :]
        weights = jnp.exp2(scores).astype(bf16)
        if same is not None:
            weights = weights * same[...]
        values = packed[:, 2 * D + low : 2 * D + high]
        single = high - low == LANES
        if single:
            values = jnp.concatenate([values, ones], 1)
        else:
            values = jnp.where(inside, values, jnp.ones_like(values))
        mixed = jnp.dot(weights, values, preferred_element_type=f32)
        left, right = mixed[:, :LANES], mixed[:, LANES:]
        before = lane < start - low
        share = 1.0 / (right if single else jnp.where(before, left, right))
        left = left * share
        if start > low:
            left = jnp.where(before, pending, left)
        pending = left if single else right * share
        if start + HEAD >= low + LANES:
            attended[:, low : low + LANES] = left.astype(bf16)


def spatial_kernel(
    step_ref, hidden_hbm, time_hbm, qkv_hbm, out_hbm,
    after_hbm,
    after_ref, hidden, modulation, gate_weight, out_weight, picker, raw, normed, packed, attended,
    sems, *parts,
):
    pairs = [(hidden_hbm, hidden), (time_hbm.at[:, 0 : 2 * D], modulation)]
    pairs += [
        (qkv_hbm.at[:, low:high], part) for low, high, part in zip(CUTS, CUTS[1:], parts)
    ]
    pairs += [(time_hbm.at[:, 2 * D : 3 * D], gate_weight), (out_hbm, out_weight)]
    copies = copies_of(pairs, sems)

    fill_picker(picker)
    activated = embed(step_ref)
    copies[0].wait()

    def normalise(rows):
        raw[rows, 0:D] = centre(hidden[rows, :].astype(f32))

    by_rows(normalise)
    copies[1].wait()
    table = jnp.dot(activated, modulation[...], preferred_element_type=f32)
    shift, scale = table[0:1, 0:D], 1.0 + table[0:1, D : 2 * D]

    def modulate(rows):
        normed[rows, :] = (raw[rows, 0:D] * scale + shift).astype(bf16)

    by_rows(modulate)
    waits = [copy.wait for copy in copies[2:6]]
    factor = project(normed, list(zip(CUTS, CUTS[1:], parts, waits)), picker, packed)
    attend(packed, factor, attended, None)
    copies[6].wait()
    copies[7].wait()
    gate = jnp.dot(activated, gate_weight[...], preferred_element_type=f32)[0:1, :]
    sent = []
    for low, width in OUT_CHUNKS:
        projected = jnp.dot(
            attended[...], out_weight[:, low : low + width], preferred_element_type=f32
        )
        after = hidden[:, low : low + width].astype(f32) + gate[:, low : low + width] * projected
        span = slice(low, low + width)
        after_ref[:, :, span] = after.astype(bf16).reshape(TPF // 2, 2, width)
        sent.append(
            pltpu.make_async_copy(
                after_ref.at[:, :, span], after_hbm.at[:, :, span], sems.at[8 + len(sent)]
            )
        )
        sent[-1].start()
    for copy in sent:
        copy.wait()


def prepare_kernel(
    step_ref, tag_ref, level_ref, time_hbm, qkv_hbm, final_hbm,
    table_hbm, early_hbm, terms_hbm, head_hbm,
    modulation, final_weight, table, terms, head_weight, sems,
):
    copies = copies_of(
        [
            (time_hbm.at[:, 3 * D : 6 * D], modulation),
            (qkv_hbm.at[:, 0:EARLY], early_hbm),
            (final_hbm, final_weight),
        ],
        sems,
    )
    activated = embed(step_ref)
    level = jnp.full((8, LANES), level_ref[tag_ref[0]], f32)
    time_value = jnp.full((8, LANES), step_ref[0], jnp.int32).astype(f32) / STEPS
    noise_scale = level * jnp.sqrt(time_value / (1.0 - time_value))
    spread = noise_scale * math.sqrt(1.0 / STEPS)
    terms[0:8, :] = noise_scale * noise_scale / (2.0 * time_value)
    terms[8:16, :] = 1.0 - time_value
    terms[16:24, :] = spread
    terms[24:32, :] = -jnp.log(spread)
    copies[0].wait()
    table[...] = jnp.dot(activated, modulation[...], preferred_element_type=f32)[0:8]
    copies[2].wait()
    padded = jnp.concatenate([final_weight[...].astype(f32), jnp.zeros((LANES - C, D), f32)], 0)
    head_weight[...] = padded.T.astype(bf16)
    results = [
        pltpu.make_async_copy(table, table_hbm, sems.at[3]),
        pltpu.make_async_copy(terms, terms_hbm, sems.at[4]),
        pltpu.make_async_copy(head_weight, head_hbm, sems.at[5]),
    ]
    for copy in results:
        copy.start()
    for copy in results:
        copy.wait()
    copies[1].wait()


def temporal_kernel(
    arrived_ref, table, early, head_weight, qkv_hbm, out_hbm,
    velocity_ref,
    picker, same, middle, value, out_weight,
    normed, packed, attended, term, after, sems,
):
    copies = copies_of(
        [
            (qkv_hbm.at[:, EARLY : 2 * D], middle),
            (qkv_hbm.at[:, 2 * D : 3 * D], value),
            (out_hbm, out_weight),
        ],
        sems,
    )
    after[...] = arrived_ref[...].reshape(TPF, D)
    fill_picker(picker)
    parity = (iota((TPF, TPF), 0) ^ iota((TPF, TPF), 1)) & 1
    same[...] = jnp.where(parity == 0, 1.0, 0.0).astype(bf16)
    shift, scale = table[0:1, 0:D], 1.0 + table[0:1, D : 2 * D]
    gate = table[0:1, 2 * D : 3 * D]

    def modulate(rows):
        normed[rows, :] = (centre(after[rows, :].astype(f32)) * scale + shift).astype(bf16)

    by_rows(modulate)

    pieces = [
        (0, EARLY, early, lambda: None),
        (EARLY, 2 * D, middle, copies[0].wait),
        (2 * D, 3 * D, value, copies[1].wait),
    ]
    factor = project(normed, pieces, picker, packed)
    attend(packed, factor, attended, same)
    copies[2].wait()
    for low, width in OUT_CHUNKS:
        term[:, low : low + width] = jnp.dot(
            attended[...], out_weight[:, low : low + width], preferred_element_type=f32
        ).astype(bf16)

    def finish(rows):
        state = after[rows, :].astype(f32) + gate * term[rows, :].astype(f32)
        normed[rows, :] = centre(state).astype(bf16)

    by_rows(finish)
    velocity_ref[...] = jnp.dot(normed[...], head_weight[...], preferred_element_type=f32)


def density_kernel(terms_ref, velocity_ref, now_ref, next_ref, log_ref, mean_ref):
    velocity = velocity_ref[...].T[0:C, :]
    factor, rest, spread, minus_log = (terms_ref[8 * row : 8 * row + 1, 0:1] for row in range(4))
    now = now_ref[0]
    drift = velocity + factor * (now + rest * velocity)
    next_mean = now - drift / STEPS
    standard = (next_ref[0] - next_mean) / spread
    log_ref[...] = (
        -0.5 * jnp.mean(standard * standard, 0, keepdims=True)
        + minus_log
        - 0.5 * math.log(2.0 * math.pi)
    )
    mean_ref[0] = next_mean


SMEM = pl.BlockSpec(memory_space=pltpu.SMEM)
HBM = pl.BlockSpec(memory_space=pltpu.HBM)
VMEM = pl.BlockSpec(memory_space=pltpu.VMEM)
work = [
    pltpu.VMEM((TPF, D), bf16),
    pltpu.VMEM((TPF, 3 * D), bf16),
    pltpu.VMEM((TPF, D), bf16),
]


def in_hbm(array):
    return pltpu.with_memory_space_constraint(array, pltpu.HBM)


def shards(
    hidden,
    latents_now,
    latents_next,
    timestep,
    version_tags,
    noise_levels,
    time_weight,
    spatial_qkv,
    spatial_out,
    temporal_qkv,
    temporal_out,
    final_weight,
):
    time_weight, temporal_qkv = in_hbm(time_weight), in_hbm(temporal_qkv)
    picker = pltpu.VMEM((2 * D, LANES), bf16)
    after_spatial = pl.pallas_call(
        spatial_kernel,
        out_shape=jax.ShapeDtypeStruct((TPF // 2, 2, D), bf16),
        in_specs=[SMEM] + [HBM] * 4,
        out_specs=HBM,
        scratch_shapes=[
            pltpu.VMEM((TPF // 2, 2, D), bf16),
            pltpu.VMEM((TPF, D), bf16),
            pltpu.VMEM((FREQ, 2 * D), bf16),
            pltpu.VMEM((FREQ, D), bf16),
            pltpu.VMEM((D, D), bf16),
            picker,
            pltpu.VMEM((TPF, D), f32),
            *work,
            pltpu.SemaphoreType.DMA((8 + len(OUT_CHUNKS),)),
            *(pltpu.VMEM((D, high - low), bf16) for low, high in zip(CUTS, CUTS[1:])),
        ],
        compiler_params=pltpu.CompilerParams(vmem_limit_bytes=40 << 20),
        cost_estimate=pl.CostEstimate(
            flops=4 << 30, bytes_accessed=14 << 20, transcendentals=1 << 20
        ),
        name="spatial",
    )(timestep, in_hbm(hidden), time_weight, in_hbm(spatial_qkv), in_hbm(spatial_out))
    arrived = lax.all_to_all(
        after_spatial, ("inner", "outer"), split_axis=0, concat_axis=0, tiled=True
    )
    table, early, terms, head_weight = pl.pallas_call(
        prepare_kernel,
        out_shape=(
            jax.ShapeDtypeStruct((8, 3 * D), f32),
            jax.ShapeDtypeStruct((D, EARLY), bf16),
            jax.ShapeDtypeStruct((32, LANES), f32),
            jax.ShapeDtypeStruct((D, LANES), bf16),
        ),
        in_specs=[SMEM] * 3 + [HBM] * 3,
        out_specs=(HBM, HBM, HBM, HBM),
        scratch_shapes=[
            pltpu.VMEM((FREQ, 3 * D), bf16),
            pltpu.VMEM((C, D), bf16),
            pltpu.VMEM((8, 3 * D), f32),
            pltpu.VMEM((32, LANES), f32),
            pltpu.VMEM((D, LANES), bf16),
            pltpu.SemaphoreType.DMA((6,)),
        ],
        compiler_params=pltpu.CompilerParams(vmem_limit_bytes=8 << 20),
        cost_estimate=pl.CostEstimate(
            flops=32 << 20, bytes_accessed=8 << 20, transcendentals=1 << 13
        ),
        name="prepare",
    )(timestep, version_tags, noise_levels, time_weight, temporal_qkv, in_hbm(final_weight))
    velocity = pl.pallas_call(
        temporal_kernel,
        out_shape=jax.ShapeDtypeStruct((TPF, LANES), f32),
        in_specs=[VMEM] * 4 + [HBM] * 2,
        out_specs=VMEM,
        scratch_shapes=[
            picker,
            pltpu.VMEM((TPF, TPF), bf16),
            pltpu.VMEM((D, 2 * D - EARLY), bf16),
            pltpu.VMEM((D, D), bf16),
            pltpu.VMEM((D, D), bf16),
            *work,
            pltpu.VMEM((TPF, D), bf16),
            pltpu.VMEM((TPF, D), bf16),
            pltpu.SemaphoreType.DMA((3,)),
        ],
        compiler_params=pltpu.CompilerParams(vmem_limit_bytes=40 << 20),
        cost_estimate=pl.CostEstimate(
            flops=4 << 30, bytes_accessed=12 << 20, transcendentals=1 << 20
        ),
        name="temporal",
    )(arrived, table, early, head_weight, temporal_qkv, in_hbm(temporal_out))
    returned = lax.all_to_all(
        velocity.reshape(TPF // 2, 2, LANES),
        ("inner", "outer"),
        split_axis=0,
        concat_axis=0,
        tiled=True,
    )
    return pl.pallas_call(
        density_kernel,
        out_shape=(
            jax.ShapeDtypeStruct((1, TPF), f32),
            jax.ShapeDtypeStruct((1, C, TPF), f32),
        ),
        in_specs=[VMEM] * 4,
        out_specs=(VMEM, VMEM),
        compiler_params=pltpu.CompilerParams(vmem_limit_bytes=4 << 20),
        name="density",
    )(terms, returned.reshape(TPF, LANES), latents_now, latents_next)


def solution(mesh):
    return jax.shard_map(
        shards,
        mesh=mesh,
        in_specs=(
            P(("inner", "outer"), None),
            P(("inner", "outer"), None, None),
            P(("inner", "outer"), None, None),
            P(),
            P(("inner", "outer")),
            P(),
            P(),
            P(),
            P(),
            P(),
            P(),
            P(),
        ),
        out_specs=(P(("inner", "outer"), None), P(("inner", "outer"), None, None)),
        check_vma=False,
    )
```
